512 devices in a mesh: patch: 128 (over z, y, core), det: 4 (over x).
Axes of the slice: x: 4, y: 8, z: 8, core: 2. Of those that a mesh axis runs over, the one named last changes fastest.
Arguments:
- strips: bfloat16 [12288, 4, 2048], P('patch', None, 'det'), may hold values from -16 to 16
- strip_patch: int32 [12288], P('patch'), may hold values from 0 to 127, as said below
- strip_row: int32 [12288], P('patch'), may hold values from 0 to 24
- strip_weight: bfloat16 [12288], P('patch'), may hold values from 0.25 to 4
- science: float32 [128, 8, 2048], P('patch', None, 'det'), may hold values from -32 to 32
Outputs:
- difference: float32 [128, 8, 2048], P('patch', None, 'det')
- coefficients: float32 [128, 4, 46], P('patch', 'det')
The draws below stay inside these ranges and needn't reach their ends.
Inputs may be any that keep to these rules, and one draw needn't show every extreme that they name: `strip_patch`: among the 96 strips of one index of patch (aligned blocks), no patch is named more than 2 times; one patch, the same for every block, is named exactly 2 times in every block.
All inputs are finite; a program needn't handle non-finite values.
Results may differ from the reference program's by a relative error of at most 0.00055.
Values may be sent and summed in bfloat16 or wider, within the bound.
No kernel may reach another device: no remote copies, remote signals or barrier semaphores. Data moves between devices by JAX's collectives and lax.ppermute only.
A program may use at most 64 MiB of HBM per device.

```python
import math
import jax
import jax.numpy as jnp
from jax import lax

W = 2048
WD = 512
BASIS = 45
TRO = 8
TR = 28
SR = 4
S_DEV = 96
STRIPS = 12288
CAP = 2
N_PATCH = 128
N_DET = 4


def pixel_noise(key, shape):
    return jax.random.normal(key, shape, jnp.float32)


def sky_field(key):
    base = jax.random.fold_in(key, 103)
    return jax.random.normal(base, (N_PATCH, TR, W), jnp.float32)


def strip_targets(key):
    base = jax.random.fold_in(key, 101)
    full_patch = jax.random.randint(jax.random.fold_in(base, 0), (), 0, N_PATCH, jnp.int32)
    block_keys = jax.random.split(jax.random.fold_in(base, 1), N_PATCH)

    def route_block(block_key):
        pick_key, order_key = jax.random.split(block_key)
        chosen_slots = jax.random.permutation(pick_key, (N_PATCH - 1) * CAP)[:S_DEV - CAP]
        others = (full_patch + 1 + chosen_slots // CAP) % N_PATCH
        values = jnp.concatenate([jnp.zeros((CAP,), jnp.int32) + full_patch, others.astype(jnp.int32)])
        return values[jax.random.permutation(order_key, S_DEV)]
    return jax.vmap(route_block)(block_keys).reshape(-1).astype(jnp.int32)


def strip_offsets(key):
    return jax.random.randint(jax.random.fold_in(key, 102), (STRIPS,), 0, TR - SR + 1, jnp.int32)


def draw_strip_patch(key, part):
    return strip_targets(key)


def draw_strip_row(key, part):
    return strip_offsets(key)


def draw_strips(key, part):
    sky = sky_field(key)
    targets = strip_targets(key)
    offsets = strip_offsets(key)
    row_index = offsets[:, None] + jnp.arange(SR, dtype=jnp.int32)[None, :]
    picked = sky[targets[:, None], row_index]
    noisy = picked + pixel_noise(jax.random.fold_in(key, 104), picked.shape)
    return jnp.clip(noisy, -16.0, 16.0).astype(jnp.bfloat16)


def draw_science(key, part):
    sky = sky_field(key)[:, 10:10 + TRO, :]
    blurred = 0.5 * sky + 0.25 * jnp.roll(sky, 1, 2) + 0.25 * jnp.roll(sky, -1, 2)
    regions = W // WD
    gains = jnp.exp(jax.random.uniform(jax.random.fold_in(key, 105), (N_PATCH, regions), jnp.float32, -0.7, 0.7))
    column_gain = jnp.repeat(gains, WD, axis=1)[:, None, :]
    noisy = column_gain * blurred + 0.3 * pixel_noise(jax.random.fold_in(key, 106), blurred.shape)
    return jnp.clip(noisy, -32.0, 32.0)


def block_levels(stream_key, dims, shards, least, top_value):
    loudness = 1.0
    for position, parts in shards:
        draws = jax.random.uniform(jax.random.fold_in(jax.random.fold_in(stream_key, 6), position), (parts,), jnp.float32, least / len(shards), top_value / len(shards))
        loudness = loudness * jnp.repeat(jnp.exp(draws), dims[position] // parts).reshape((-1,) + (1,) * (len(dims) - 1 - position))
    return loudness


def setup_inputs(seed: int = 0) -> dict:
    key_list = jax.random.split(jax.random.key(seed), 6)
    strips = draw_strips(jax.random.fold_in(key_list[5], 71), 0)
    strip_patch = draw_strip_patch(jax.random.fold_in(key_list[5], 71), 0)
    strip_row = draw_strip_row(jax.random.fold_in(key_list[5], 71), 0)
    strip_weight = jnp.clip(jnp.exp(math.log(4.0) - 2.7725887 * jax.random.uniform(key_list[3], (STRIPS,), jnp.float32) ** block_levels(key_list[3], (STRIPS,), ((0, 128),), -0.2, 0.2)), 0.25, 4.0).astype(jnp.bfloat16)
    science = draw_science(jax.random.fold_in(key_list[5], 71), 0)
    return {"strips": strips, "strip_patch": strip_patch, "strip_row": strip_row, "strip_weight": strip_weight, "science": science}


SIGMAS = (0.7, 1.5, 3.0)
RIDGE = 0.01

def basis_tables():
    tap_offsets = jnp.arange(21, dtype=jnp.float32) - 10.0
    profiles = []
    for gauss_width in SIGMAS:
        for degree in range(5):
            scaled = tap_offsets / gauss_width
            profile = scaled ** degree * jnp.exp(-0.5 * scaled * scaled)
            profiles.append(profile / jnp.sqrt(jnp.sum(profile * profile)))
    kernels = jnp.stack(profiles)
    col_pick = []
    row_pick = []
    for s in range(3):
        for i in range(5):
            for j in range(5 - i):
                col_pick.append(5 * s + i)
                row_pick.append(5 * s + j)
    return (kernels, col_pick, row_pick)

def row_matrices(kernels, row_pick, out_rows, in_rows):
    reach = jnp.arange(in_rows, dtype=jnp.int32)[None, :] - jnp.arange(out_rows, dtype=jnp.int32)[:, None]
    onehot = (reach[:, :, None] == jnp.arange(21, dtype=jnp.int32)[None, None, :]).astype(jnp.float32)
    chosen = jnp.stack([kernels[r] for r in row_pick])
    return jnp.einsum('ka,ota->kot', chosen, onehot, precision=lax.Precision.HIGHEST)

def solve_normal(normal, target):
    unknowns = normal.shape[0]
    ridge_shift = RIDGE * jnp.trace(normal) / unknowns
    system = normal + ridge_shift * jnp.eye(unknowns, dtype=normal.dtype)
    factor = jnp.linalg.cholesky(system)
    forward = lax.linalg.triangular_solve(factor, target[:, None], left_side=True, lower=True)
    backward = lax.linalg.triangular_solve(factor, forward, left_side=True, lower=True, transpose_a=True)
    return backward[:, 0]

def reference(strips, strip_patch, strip_row, strip_weight, science):
    columns = strips.shape[2]
    det_width = columns // N_DET

    def add_block(running, item):
        strip_block, targets, offsets, weights = item
        numerator, coverage = running
        weighted = strip_block.astype(jnp.float32) * weights.astype(jnp.float32)[:, None, None]
        row_index = (targets * TR + offsets)[:, None] + jnp.arange(SR, dtype=jnp.int32)[None, :]
        numerator = numerator.at[row_index.reshape(-1)].add(weighted.reshape(-1, columns))
        coverage = coverage.at[row_index.reshape(-1)].add(jnp.repeat(weights.astype(jnp.float32), SR))
        return ((numerator, coverage), None)
    start = (jnp.zeros((N_PATCH * TR, columns), jnp.float32), jnp.zeros((N_PATCH * TR,), jnp.float32))
    items = (strips.reshape(N_PATCH, S_DEV, SR, columns), strip_patch.reshape(N_PATCH, S_DEV), strip_row.reshape(N_PATCH, S_DEV), strip_weight.reshape(N_PATCH, S_DEV))
    (numerator, coverage), unused = lax.scan(add_block, start, items)
    template = (numerator / (1.0 + coverage)[:, None]).reshape(N_PATCH, TR, columns)
    kernels, col_pick, row_pick = basis_tables()
    rowmats = row_matrices(kernels, row_pick, TRO, TR)

    def fit_patch(item):
        template_one, science_image = item
        padded = jnp.pad(template_one, ((0, 0), (10, 10)))
        shifted = jnp.stack([padded[:, a:a + columns] for a in range(21)])
        colconv = jnp.einsum('ka,atw->ktw', kernels, shifted, precision=lax.Precision.HIGHEST)
        picked = jnp.stack([colconv[c] for c in col_pick])
        basis_images = jnp.einsum('kot,ktw->kow', rowmats, picked, precision=lax.Precision.HIGHEST)
        pixels = TRO * det_width
        per_det = basis_images.reshape(BASIS, TRO, N_DET, det_width).transpose(2, 0, 1, 3).reshape(N_DET, BASIS, pixels)
        design = jnp.concatenate([per_det, jnp.ones((N_DET, 1, pixels), jnp.float32)], axis=1)
        sci = science_image.reshape(TRO, N_DET, det_width).transpose(1, 0, 2).reshape(N_DET, pixels)
        normal = jnp.einsum('dkp,dlp->dkl', design, design, precision=lax.Precision.HIGHEST)
        target = jnp.einsum('dkp,dp->dk', design, sci, precision=lax.Precision.HIGHEST)
        fitted = jax.vmap(solve_normal)(normal, target)
        model_image = jnp.einsum('dk,dkp->dp', fitted, design, precision=lax.Precision.HIGHEST)
        residual = (sci - model_image).reshape(N_DET, TRO, det_width).transpose(1, 0, 2).reshape(TRO, columns)
        return (fitted, residual)
    coefficients, difference = lax.map(fit_patch, (template, science))
    return (difference, coefficients)
```

```python
import jax
import jax.numpy as jnp
import numpy as np
from jax import lax
from jax.experimental import pallas as pl
from jax.experimental.pallas import tpu as pltpu
from jax.sharding import PartitionSpec as P

BASIS = 45
SIGMAS = (0.7, 1.5, 3.0)
RIDGE = 0.01
TAPS = 21
REACH = 10
ROWS = 8
TROWS = 32
SLOTS = 8
EXTRA = 128
ONE = 32
KP = 48
UNKNOWNS = BASIS + 1
F32 = jnp.float32
BF16 = jnp.bfloat16


def tap_table():
    offsets = np.arange(TAPS, dtype=np.float64) - REACH
    profiles = []
    for width in SIGMAS:
        for degree in range(5):
            scaled = offsets / width
            profile = scaled**degree * np.exp(-0.5 * scaled * scaled)
            profiles.append(profile / np.sqrt(np.sum(profile * profile)))
    table = np.zeros((ROWS, KP, TAPS, TROWS))
    k = 0
    for s in range(3):
        for i in range(5):
            for j in range(5 - i):
                kernel = np.outer(profiles[5 * s + i], profiles[5 * s + j])
                for o in range(ROWS):
                    table[o, k, :, o : o + TAPS] = kernel
                k += 1
    table = table.reshape(ROWS * KP, TAPS * TROWS).astype(np.float32)
    high = table.astype(BF16)
    low = (table - high.astype(np.float32)).astype(BF16)
    return high, low


def iota(shape, dim):
    return lax.broadcasted_iota(jnp.int32, shape, dim)


def split(x):
    high = x.astype(BF16)
    return high, (x - high.astype(F32)).astype(BF16)


def pack_kernel(strips_ref, patch_ref, row_ref, weight_ref, out_ref):
    count = patch_ref.shape[1]
    lines = strips_ref.shape[0]
    columns = strips_ref.shape[1]
    reps = lines // count
    first, second = iota((count, count), 0), iota((count, count), 1)
    patch = jnp.broadcast_to(patch_ref[...], (count, count))
    patch_col = jnp.sum(jnp.where(first == second, patch, 0).astype(F32), axis=1, keepdims=True)
    earlier = (patch.astype(F32) == patch_col) & (first < second)
    occurrence = jnp.sum(jnp.where(earlier, 1.0, 0.0), axis=0, keepdims=True)
    place = 2.0 * patch_ref[...].astype(F32) + occurrence
    spread = (iota((count, lines), 1) // reps == iota((count, lines), 0)).astype(F32).astype(BF16)
    wide = jnp.dot(
        jnp.broadcast_to(place, (8, count)).astype(BF16), spread, preferred_element_type=F32
    )[:1]
    key = wide.astype(jnp.int32) * reps + iota((1, lines), 1) % reps
    here = iota((lines, count), 0) // reps == iota((lines, count), 1)
    row = jnp.sum(
        jnp.where(here, row_ref[...].astype(F32), 0.0), axis=1, keepdims=True
    ).astype(jnp.int32)
    weight = jnp.sum(jnp.where(here, weight_ref[...], 0.0), axis=1, keepdims=True)
    lane = iota((lines, EXTRA), 1)
    at = row + iota((lines, EXTRA), 0) % reps
    extra = jnp.where(lane == at, weight, jnp.where(lane == ONE, 1.0, 0.0)).astype(BF16)
    strips = strips_ref[...]
    total = out_ref.shape[0]
    step = 256
    for base in range(0, total, step):
        pick = (iota((step, lines), 0) + base == key).astype(F32).astype(BF16)
        out_ref[base : base + step, :columns] = jnp.dot(
            pick, strips, preferred_element_type=F32
        ).astype(BF16)
        out_ref[base : base + step, columns:] = jnp.dot(
            pick, extra, preferred_element_type=F32
        ).astype(BF16)


def template_kernel(received_ref, template_ref, first_ref, last_ref):
    columns = template_ref.shape[1]
    spread = received_ref[:, columns:]
    sums = lax.dot_general(
        spread, received_ref[...], (((0,), (0,)), ((), ())), preferred_element_type=F32
    )[:TROWS]
    coverage = sums[:, columns + ONE : columns + ONE + 1]
    template = sums[:, :columns] / (1.0 + coverage)
    template_ref[...] = template
    first_ref[...] = template[:, :128]
    last_ref[...] = template[:, columns - 128 :]


def fit_kernel(
    template_ref, before_ref, after_ref, science_ref, high_ref, low_ref,
    difference_ref, coefficients_ref, design_ref, parts_ref,
):
    columns = template_ref.shape[1]
    padded = jnp.concatenate([before_ref[...], template_ref[...], after_ref[...]], axis=1)
    upper, lower = split(padded)
    left = 128 - REACH
    upper_taps = jnp.concatenate([upper[:, left + a : left + a + columns] for a in range(TAPS)])
    lower_taps = jnp.concatenate([lower[:, left + a : left + a + columns] for a in range(TAPS)])
    basis = (
        jnp.dot(high_ref[...], upper_taps, preferred_element_type=F32)
        + jnp.dot(high_ref[...], lower_taps, preferred_element_type=F32)
        + jnp.dot(low_ref[...], upper_taps, preferred_element_type=F32)
    )
    science = science_ref[...]
    place = iota((KP, columns), 0)
    for o in range(ROWS):
        image = basis[o * KP : (o + 1) * KP]
        image = jnp.where(place == BASIS, 1.0, image)
        image = jnp.where(place == UNKNOWNS, science[o : o + 1], image)
        design_ref[o] = image
        image_high, image_low = split(image)
        parts_ref[:KP, o * columns : (o + 1) * columns] = image_high
        parts_ref[KP:, o * columns : (o + 1) * columns] = image_low
    parts = parts_ref[...]
    gram = lax.dot_general(
        parts, parts, (((1,), (1,)), ((), ())), preferred_element_type=F32
    )
    half = gram[:KP] + gram[KP:]
    system = half[:, :KP] + half[:, KP:]
    down, across = iota((KP, KP), 0), iota((KP, KP), 1)
    diagonal = (down == across) & (down < UNKNOWNS)
    trace = jnp.sum(jnp.where(diagonal, system, 0.0))
    system = system + jnp.where(diagonal, RIDGE * trace / UNKNOWNS, 0.0)
    line = iota((KP, 1), 0)
    for k in range(UNKNOWNS):
        pivot = system[k : k + 1, :] * (1.0 / system[k : k + 1, k : k + 1])
        column = jnp.where(line == k, 0.0, system[:, k : k + 1])
        system = system - column * pivot
    scale = jnp.sum(jnp.where(diagonal, system, 0.0), axis=1, keepdims=True)
    fitted = jnp.where(
        line < UNKNOWNS, system[:, UNKNOWNS : UNKNOWNS + 1] / jnp.where(line < UNKNOWNS, scale, 1.0), 0.0
    )
    coefficients_ref[...] = jnp.sum(jnp.where(down == across, fitted, 0.0), axis=0, keepdims=True)[
        :, :UNKNOWNS
    ]
    for o in range(ROWS):
        model = jnp.sum(design_ref[o] * fitted, axis=0, keepdims=True)
        difference_ref[o : o + 1, :] = science[o : o + 1] - model


def call(kernel, outs, *args, scratch=()):
    return pl.pallas_call(
        kernel,
        out_shape=[jax.ShapeDtypeStruct(shape, dtype) for shape, dtype in outs],
        scratch_shapes=scratch,
        name=kernel.__name__,
    )(*args)


def body(strips, strip_patch, strip_row, strip_weight, science):
    peers = lax.axis_size("patch")
    count, lines, columns = strips.shape
    (payload,) = call(
        pack_kernel,
        [((peers * SLOTS, columns + EXTRA), BF16)],
        strips.reshape(count * lines, columns),
        strip_patch[None, :],
        strip_row[None, :],
        strip_weight.astype(F32)[None, :],
    )
    received = lax.all_to_all(
        payload.reshape(peers, SLOTS, columns + EXTRA), "patch", split_axis=0, concat_axis=0, tiled=True
    ).reshape(peers * SLOTS, columns + EXTRA)
    template, first, last = call(
        template_kernel,
        [((TROWS, columns), F32), ((TROWS, 128), F32), ((TROWS, 128), F32)],
        received,
    )
    devices = lax.axis_size("det")
    up = [(i, i + 1) for i in range(devices - 1)]
    before = lax.ppermute(last, "det", up)
    after = lax.ppermute(first, "det", [(j, i) for i, j in up])
    high, low = tap_table()
    difference, coefficients = call(
        fit_kernel,
        [((ROWS, columns), F32), ((1, UNKNOWNS), F32)],
        template,
        before,
        after,
        science[0],
        jnp.asarray(high),
        jnp.asarray(low),
        scratch=[
            pltpu.VMEM((ROWS, KP, columns), F32),
            pltpu.VMEM((2 * KP, ROWS * columns), BF16),
        ],
    )
    return (difference[None], coefficients[None])


def solution(mesh):
    placed = (P("patch", None, "det"), P("patch"), P("patch"), P("patch"), P("patch", None, "det"))
    return jax.shard_map(
        body,
        mesh=mesh,
        in_specs=placed,
        out_specs=(P("patch", None, "det"), P("patch", "det", None)),
        check_vma=False,
    )
```

```python
import jax
import jax.numpy as jnp
import numpy as np
from jax import lax
from jax.experimental import pallas as pl
from jax.experimental.pallas import tpu as pltpu
from jax.sharding import PartitionSpec as P

BASIS = 45
SIGMAS = (0.7, 1.5, 3.0)
RIDGE = 0.01
TAPS = 21
REACH = 10
ROWS = 8
TROWS = 32
SLOTS = 8
EXTRA = 128
SPREAD = 32
ONE = 64
KP = 48
UNKNOWNS = BASIS + 1
F32 = jnp.float32
BF16 = jnp.bfloat16


def tap_table():
    offsets = np.arange(TAPS, dtype=np.float64) - REACH
    profiles = []
    for width in SIGMAS:
        for degree in range(5):
            scaled = offsets / width
            profile = scaled**degree * np.exp(-0.5 * scaled * scaled)
            profiles.append(profile / np.sqrt(np.sum(profile * profile)))
    table = np.zeros((ROWS, KP, TAPS, TROWS))
    k = 0
    for s in range(3):
        for i in range(5):
            for j in range(5 - i):
                kernel = np.outer(profiles[5 * s + i], profiles[5 * s + j])
                for o in range(ROWS):
                    table[o, k, :, o : o + TAPS] = kernel
                k += 1
    table = table.reshape(ROWS * KP, TAPS * TROWS).astype(np.float32)
    high = table.astype(BF16)
    low = (table - high.astype(np.float32)).astype(BF16)
    return high, low


def iota(shape, dim):
    return lax.broadcasted_iota(jnp.int32, shape, dim)


def split(x):
    high = x.astype(BF16)
    return high, (x - high.astype(F32)).astype(BF16)


def pick_rows(key, base, step):
    shape = (step, key.shape[1])
    return (iota(shape, 0) + base == key).astype(F32).astype(BF16)


def pack_kernel(strips_ref, patch_ref, row_ref, weight_ref, out_ref, key_ref, extra_ref):
    count = patch_ref.shape[1]
    lines, columns = strips_ref.shape
    reps = lines // count
    first, second = iota((count, count), 0), iota((count, count), 1)
    patch = jnp.broadcast_to(patch_ref[...], (count, count))
    patch_col = jnp.sum(jnp.where(first == second, patch, 0).astype(F32), axis=1, keepdims=True)
    earlier = (patch.astype(F32) == patch_col) & (first < second)
    occurrence = jnp.sum(jnp.where(earlier, 1.0, 0.0), axis=0, keepdims=True)
    place = 2.0 * patch_ref[...].astype(F32) + occurrence
    spread = (iota((count, lines), 1) // reps == iota((count, lines), 0)).astype(F32).astype(BF16)
    wide = jnp.dot(
        jnp.broadcast_to(place, (8, count)).astype(BF16), spread, preferred_element_type=F32
    )[:1]
    key = wide.astype(jnp.int32) * reps + iota((1, lines), 1) % reps
    key_ref[...] = key
    strips = strips_ref[...]
    step = 256
    for base in range(0, out_ref.shape[0], step):
        out_ref[base : base + step, :] = jnp.dot(
            pick_rows(key, base, step), strips, preferred_element_type=F32
        ).astype(BF16)
    here = iota((lines, count), 0) // reps == iota((lines, count), 1)
    row = jnp.sum(
        jnp.where(here, row_ref[...].astype(F32), 0.0), axis=1, keepdims=True
    ).astype(jnp.int32)
    weight = jnp.sum(jnp.where(here, weight_ref[...].astype(F32), 0.0), axis=1, keepdims=True)
    lane = iota((lines, EXTRA), 1)
    at = row + iota((lines, EXTRA), 0) % reps + SPREAD
    extra_ref[...] = jnp.where(lane == at, weight, jnp.where(lane == ONE, 1.0, 0.0)).astype(BF16)


def edge_kernel(key_ref, extra_ref, before_ref, after_ref, unused_ref, out_ref):
    lane = iota(extra_ref.shape, 1)
    extra = jnp.where(
        lane < REACH,
        after_ref[...].astype(F32),
        jnp.where(lane >= EXTRA - REACH, before_ref[...].astype(F32), extra_ref[...].astype(F32)),
    ).astype(BF16)
    key = key_ref[...]
    step = 256
    for base in range(0, out_ref.shape[0], step):
        out_ref[base : base + step, :] = jnp.dot(
            pick_rows(key, base, step), extra, preferred_element_type=F32
        ).astype(BF16)


def fit_kernel(
    received_ref, science_ref, high_ref, low_ref,
    difference_ref, coefficients_ref, design_ref, parts_ref,
):
    columns = science_ref.shape[1]
    sums = lax.dot_general(
        received_ref[:, columns:],
        received_ref[...],
        (((0,), (0,)), ((), ())),
        preferred_element_type=F32,
    )[SPREAD : SPREAD + TROWS]
    coverage = sums[:, columns + ONE : columns + ONE + 1]
    template = sums / (1.0 + coverage)
    edges = template[:, columns:]
    upper, lower = split(jnp.concatenate([edges, template[:, :columns], edges], axis=1))
    left = EXTRA - REACH
    upper_taps = jnp.concatenate([upper[:, left + a : left + a + columns] for a in range(TAPS)])
    lower_taps = jnp.concatenate([lower[:, left + a : left + a + columns] for a in range(TAPS)])
    basis = (
        jnp.dot(high_ref[...], upper_taps, preferred_element_type=F32)
        + jnp.dot(high_ref[...], lower_taps, preferred_element_type=F32)
        + jnp.dot(low_ref[...], upper_taps, preferred_element_type=F32)
    )
    science = science_ref[...]
    place = iota((KP, columns), 0)
    for o in range(ROWS):
        image = basis[o * KP : (o + 1) * KP]
        image = jnp.where(place == BASIS, 1.0, image)
        image = jnp.where(place == UNKNOWNS, science[o : o + 1], image)
        design_ref[o] = image
        image_high, image_low = split(image)
        parts_ref[:KP, o * columns : (o + 1) * columns] = image_high
        parts_ref[KP:, o * columns : (o + 1) * columns] = image_low
    parts = parts_ref[...]
    gram = lax.dot_general(parts, parts, (((1,), (1,)), ((), ())), preferred_element_type=F32)
    half = gram[:KP] + gram[KP:]
    system = half[:, :KP] + half[:, KP:]
    down, across = iota((KP, KP), 0), iota((KP, KP), 1)
    diagonal = (down == across) & (down < UNKNOWNS)
    trace = jnp.sum(jnp.where(diagonal, system, 0.0))
    system = system + jnp.where(diagonal, RIDGE * trace / UNKNOWNS, 0.0)
    groups = [system[g : g + 8] for g in range(0, KP, 8)]
    line = iota((8, KP), 0)
    for k in range(0, UNKNOWNS, 2):
        at, own = k % 8, k // 8
        col0 = [jnp.broadcast_to(g[:, k : k + 1], (8, KP)) for g in groups]
        col1 = [jnp.broadcast_to(g[:, k + 1 : k + 2], (8, KP)) for g in groups]
        row0, row1 = groups[own][at : at + 1], groups[own][at + 1 : at + 2]
        a, b = col0[own][at : at + 1], col0[own][at + 1 : at + 2]
        d = col1[own][at + 1 : at + 2]
        inverse = 1.0 / (a * d - b * b)
        new0 = (d * row0 - b * row1) * inverse
        new1 = (a * row1 - b * row0) * inverse
        groups = [g - c0 * new0 - c1 * new1 for g, c0, c1 in zip(groups, col0, col1)]
        groups[own] = jnp.where(
            line == at, new0, jnp.where(line == at + 1, new1, groups[own])
        )
    system = jnp.concatenate(groups)
    fitted = jnp.where(down[:, :1] < UNKNOWNS, system[:, UNKNOWNS : UNKNOWNS + 1], 0.0)
    coefficients_ref[...] = jnp.sum(jnp.where(down == across, fitted, 0.0), axis=0, keepdims=True)[
        :, :UNKNOWNS
    ]
    for o in range(ROWS):
        model = jnp.sum(design_ref[o] * fitted, axis=0, keepdims=True)
        difference_ref[o : o + 1, :] = science[o : o + 1] - model


def call(kernel, outs, *args, **options):
    return pl.pallas_call(
        kernel,
        out_shape=[jax.ShapeDtypeStruct(shape, dtype) for shape, dtype in outs],
        name=kernel.__name__,
        **options,
    )(*args)


def pack(strips, strip_patch, strip_row, strip_weight, peers):
    lines, columns = strips.shape
    return call(
        pack_kernel,
        [
            ((peers * SLOTS, columns + EXTRA), BF16),
            ((1, lines), jnp.int32),
            ((lines, EXTRA), BF16),
        ],
        strips,
        strip_patch[None, :],
        strip_row[None, :],
        strip_weight[None, :],
        grid=(1,),
        out_specs=[
            pl.BlockSpec((peers * SLOTS, columns), lambda i: (0, 0)),
            pl.BlockSpec((1, lines), lambda i: (0, 0)),
            pl.BlockSpec((lines, EXTRA), lambda i: (0, 0)),
        ],
        cost_estimate=pl.CostEstimate(flops=10**9, bytes_accessed=2 * 10**6, transcendentals=0),
    )


def add_edges(payload, key, extra, before, after):
    rows, wide = payload.shape
    lines = key.shape[1]
    block = pl.BlockSpec((rows, EXTRA), lambda i: (0, wide // EXTRA - 1))
    whole = pl.BlockSpec((lines, EXTRA), lambda i: (0, 0))
    (payload,) = call(
        edge_kernel,
        [(payload.shape, BF16)],
        key,
        extra,
        before,
        after,
        payload,
        grid=(1,),
        in_specs=[pl.BlockSpec((1, lines), lambda i: (0, 0)), whole, whole, whole]
        + [pl.BlockSpec(memory_space=pl.ANY)],
        out_specs=[block],
        input_output_aliases={4: 0},
    )
    return payload


def fit(received, science):
    rows, columns = science.shape
    high, low = tap_table()
    return call(
        fit_kernel,
        [((rows, columns), F32), ((1, UNKNOWNS), F32)],
        received,
        science,
        jnp.asarray(high),
        jnp.asarray(low),
        scratch_shapes=[
            pltpu.VMEM((ROWS, KP, columns), F32),
            pltpu.VMEM((2 * KP, ROWS * columns), BF16),
        ],
    )


def body(strips, strip_patch, strip_row, strip_weight, science):
    peers = lax.axis_size("patch")
    devices = lax.axis_size("det")
    count, lines, columns = strips.shape
    up = [(i, i + 1) for i in range(devices - 1)]
    down = [(j, i) for i, j in up]
    last = strips[:, :, columns - EXTRA :].reshape(count * lines, EXTRA)
    first = strips[:, :, :EXTRA].reshape(count * lines, EXTRA)
    before = lax.ppermute(last, "det", up)
    after = lax.ppermute(first, "det", down)
    payload, key, extra = pack(
        strips.reshape(count * lines, columns), strip_patch, strip_row, strip_weight, peers
    )
    payload = add_edges(payload, key, extra, before, after)
    received = lax.all_to_all(
        payload.reshape(peers, SLOTS, columns + EXTRA),
        "patch",
        split_axis=0,
        concat_axis=0,
        tiled=True,
    ).reshape(peers * SLOTS, columns + EXTRA)
    difference, coefficients = fit(received, science[0])
    return (difference[None], coefficients[None])


def solution(mesh):
    placed = (P("patch", None, "det"), P("patch"), P("patch"), P("patch"), P("patch", None, "det"))
    return jax.shard_map(
        body,
        mesh=mesh,
        in_specs=placed,
        out_specs=(P("patch", None, "det"), P("patch", "det", None)),
        check_vma=False,
    )
```

```python
import jax
import jax.numpy as jnp
import numpy as np
from jax import lax
from jax.experimental import pallas as pl
from jax.experimental.pallas import tpu as pltpu
from jax.sharding import PartitionSpec as P

BASIS = 45
SIGMAS = (0.7, 1.5, 3.0)
RIDGE = 0.01
TAPS = 21
REACH = 10
ROWS = 8
TROWS = 32
SLOTS = 8
EXTRA = 128
SPREAD = 32
ONE = 64
KP = 48
UNKNOWNS = BASIS + 1
VMEM_LIMIT = 12 * 2**20
F32 = jnp.float32
BF16 = jnp.bfloat16


def tap_table():
    offsets = np.arange(TAPS, dtype=np.float64) - REACH
    profiles = []
    for width in SIGMAS:
        for degree in range(5):
            scaled = offsets / width
            profile = scaled**degree * np.exp(-0.5 * scaled * scaled)
            profiles.append(profile / np.sqrt(np.sum(profile * profile)))
    table = np.zeros((ROWS, KP, TAPS, TROWS))
    k = 0
    for s in range(3):
        for i in range(5):
            for j in range(5 - i):
                kernel = np.outer(profiles[5 * s + i], profiles[5 * s + j])
                for o in range(ROWS):
                    table[o, k, :, o : o + TAPS] = kernel
                k += 1
    table = table.reshape(ROWS * KP, TAPS * TROWS).astype(np.float32)
    high = table.astype(BF16)
    low = (table - high.astype(np.float32)).astype(BF16)
    return high, low


def iota(shape, dim):
    return lax.broadcasted_iota(jnp.int32, shape, dim)


def split(x):
    high = x.astype(BF16)
    return high, (x - high.astype(F32)).astype(BF16)


def pick_rows(key, base, step):
    shape = (step, key.shape[1])
    return (iota(shape, 0) + base == key).astype(F32).astype(BF16)


def pack_kernel(strips_ref, notes_ref, out_ref, key_ref, extra_ref):
    count = notes_ref.shape[1]
    patch_row, row_row, weight_row = (notes_ref[i : i + 1, :] for i in range(3))
    lines, columns = strips_ref.shape
    reps = lines // count
    first, second = iota((count, count), 0), iota((count, count), 1)
    patch = jnp.broadcast_to(patch_row, (count, count))
    patch_col = jnp.sum(jnp.where(first == second, patch, 0.0), axis=1, keepdims=True)
    earlier = (patch == patch_col) & (first < second)
    occurrence = jnp.sum(jnp.where(earlier, 1.0, 0.0), axis=0, keepdims=True)
    place = 2.0 * patch_row + occurrence
    spread = (iota((count, lines), 1) // reps == iota((count, lines), 0)).astype(F32).astype(BF16)
    wide = jnp.dot(
        jnp.broadcast_to(place, (8, count)).astype(BF16), spread, preferred_element_type=F32
    )[:1]
    key = wide.astype(jnp.int32) * reps + iota((1, lines), 1) % reps
    key_ref[...] = key
    strips = strips_ref[...]
    step = 256
    for base in range(0, out_ref.shape[0], step):
        out_ref[base : base + step, :] = jnp.dot(
            pick_rows(key, base, step), strips, preferred_element_type=F32
        ).astype(BF16)
    here = iota((lines, count), 0) // reps == iota((lines, count), 1)
    row = jnp.sum(jnp.where(here, row_row, 0.0), axis=1, keepdims=True).astype(jnp.int32)
    weight = jnp.sum(jnp.where(here, weight_row, 0.0), axis=1, keepdims=True)
    lane = iota((lines, EXTRA), 1)
    at = row + iota((lines, EXTRA), 0) % reps + SPREAD
    extra_ref[...] = jnp.where(lane == at, weight, jnp.where(lane == ONE, 1.0, 0.0)).astype(BF16)


def edge_kernel(key_ref, extra_ref, before_ref, after_ref, unused_ref, out_ref):
    lane = iota(extra_ref.shape, 1)
    extra = jnp.where(
        lane < REACH,
        after_ref[...].astype(F32),
        jnp.where(lane >= EXTRA - REACH, before_ref[...].astype(F32), extra_ref[...].astype(F32)),
    ).astype(BF16)
    key = key_ref[...]
    step = 256
    for base in range(0, out_ref.shape[0], step):
        out_ref[base : base + step, :] = jnp.dot(
            pick_rows(key, base, step), extra, preferred_element_type=F32
        ).astype(BF16)


def fit_kernel(
    received_ref, science_ref, high_ref, low_ref,
    difference_ref, coefficients_ref, design_ref, parts_ref,
):
    columns = science_ref.shape[1]
    sums = lax.dot_general(
        received_ref[:, columns:],
        received_ref[...],
        (((0,), (0,)), ((), ())),
        preferred_element_type=F32,
    )[SPREAD : SPREAD + TROWS]
    coverage = sums[:, columns + ONE : columns + ONE + 1]
    template = sums / (1.0 + coverage)
    edges = template[:, columns:]
    upper, lower = split(jnp.concatenate([edges, template[:, :columns], edges], axis=1))
    left = EXTRA - REACH
    upper_taps = jnp.concatenate([upper[:, left + a : left + a + columns] for a in range(TAPS)])
    lower_taps = jnp.concatenate([lower[:, left + a : left + a + columns] for a in range(TAPS)])
    basis = (
        jnp.dot(high_ref[...], upper_taps, preferred_element_type=F32)
        + jnp.dot(high_ref[...], lower_taps, preferred_element_type=F32)
        + jnp.dot(low_ref[...], upper_taps, preferred_element_type=F32)
    )
    science = science_ref[...]
    place = iota((KP, columns), 0)
    for o in range(ROWS):
        image = basis[o * KP : (o + 1) * KP]
        image = jnp.where(place == BASIS, 1.0, image)
        image = jnp.where(place == UNKNOWNS, science[o : o + 1], image)
        design_ref[o] = image
        image_high, image_low = split(image)
        parts_ref[:KP, o * columns : (o + 1) * columns] = image_high
        parts_ref[KP:, o * columns : (o + 1) * columns] = image_low
    parts = parts_ref[...]
    gram = lax.dot_general(parts, parts, (((1,), (1,)), ((), ())), preferred_element_type=F32)
    half = gram[:KP] + gram[KP:]
    system = half[:, :KP] + half[:, KP:]
    down, across = iota((KP, KP), 0), iota((KP, KP), 1)
    diagonal = (down == across) & (down < UNKNOWNS)
    trace = jnp.sum(jnp.where(diagonal, system, 0.0))
    system = system + jnp.where(diagonal, RIDGE * trace / UNKNOWNS, 0.0)
    groups = [system[g : g + 8] for g in range(0, KP, 8)]
    line = iota((8, KP), 0)
    for k in range(0, UNKNOWNS, 2):
        at, own = k % 8, k // 8
        col0 = [jnp.broadcast_to(g[:, k : k + 1], (8, KP)) for g in groups]
        col1 = [jnp.broadcast_to(g[:, k + 1 : k + 2], (8, KP)) for g in groups]
        row0, row1 = groups[own][at : at + 1], groups[own][at + 1 : at + 2]
        a, b = col0[own][at : at + 1], col0[own][at + 1 : at + 2]
        d = col1[own][at + 1 : at + 2]
        inverse = 1.0 / (a * d - b * b)
        new0 = (d * row0 - b * row1) * inverse
        new1 = (a * row1 - b * row0) * inverse
        groups = [g - c0 * new0 - c1 * new1 for g, c0, c1 in zip(groups, col0, col1)]
        groups[own] = jnp.where(
            line == at, new0, jnp.where(line == at + 1, new1, groups[own])
        )
    system = jnp.concatenate(groups)
    fitted = jnp.where(down[:, :1] < UNKNOWNS, system[:, UNKNOWNS : UNKNOWNS + 1], 0.0)
    coefficients_ref[...] = jnp.sum(jnp.where(down == across, fitted, 0.0), axis=0, keepdims=True)[
        :, :UNKNOWNS
    ]
    for o in range(ROWS):
        model = jnp.sum(design_ref[o] * fitted, axis=0, keepdims=True)
        difference_ref[o : o + 1, :] = science[o : o + 1] - model


def call(kernel, outs, *args, **options):
    return pl.pallas_call(
        kernel,
        out_shape=[jax.ShapeDtypeStruct(shape, dtype) for shape, dtype in outs],
        name=kernel.__name__,
        compiler_params=pltpu.CompilerParams(vmem_limit_bytes=VMEM_LIMIT),
        **options,
    )(*args)


def pack(strips, strip_patch, strip_row, strip_weight, peers):
    lines, columns = strips.shape
    notes = jnp.stack([x.astype(F32) for x in (strip_patch, strip_row, strip_weight)])
    return call(
        pack_kernel,
        [
            ((peers * SLOTS, columns + EXTRA), BF16),
            ((1, lines), jnp.int32),
            ((lines, EXTRA), BF16),
        ],
        strips,
        notes,
        grid=(1,),
        out_specs=[
            pl.BlockSpec((peers * SLOTS, columns), lambda i: (0, 0)),
            pl.BlockSpec((1, lines), lambda i: (0, 0)),
            pl.BlockSpec((lines, EXTRA), lambda i: (0, 0)),
        ],
        cost_estimate=pl.CostEstimate(flops=10**9, bytes_accessed=2 * 10**6, transcendentals=0),
    )


def add_edges(payload, key, extra, before, after):
    rows, wide = payload.shape
    lines = key.shape[1]
    block = pl.BlockSpec((rows, EXTRA), lambda i: (0, wide // EXTRA - 1))
    whole = pl.BlockSpec((lines, EXTRA), lambda i: (0, 0))
    (payload,) = call(
        edge_kernel,
        [(payload.shape, BF16)],
        key,
        extra,
        before,
        after,
        payload,
        grid=(1,),
        in_specs=[pl.BlockSpec((1, lines), lambda i: (0, 0)), whole, whole, whole]
        + [pl.BlockSpec(memory_space=pl.ANY)],
        out_specs=[block],
        input_output_aliases={4: 0},
    )
    return payload


def fit(received, science):
    rows, columns = science.shape
    high, low = tap_table()
    return call(
        fit_kernel,
        [((rows, columns), F32), ((1, UNKNOWNS), F32)],
        received,
        science,
        jnp.asarray(high),
        jnp.asarray(low),
        scratch_shapes=[
            pltpu.VMEM((ROWS, KP, columns), F32),
            pltpu.VMEM((2 * KP, ROWS * columns), BF16),
        ],
    )


def body(strips, strip_patch, strip_row, strip_weight, science):
    peers = lax.axis_size("patch")
    devices = lax.axis_size("det")
    count, lines, columns = strips.shape
    up = [(i, i + 1) for i in range(devices - 1)]
    down = [(j, i) for i, j in up]
    last = strips[:, :, columns - EXTRA :].reshape(count * lines, EXTRA)
    first = strips[:, :, :EXTRA].reshape(count * lines, EXTRA)
    before = lax.ppermute(last, "det", up)
    after = lax.ppermute(first, "det", down)
    payload, key, extra = pack(
        strips.reshape(count * lines, columns), strip_patch, strip_row, strip_weight, peers
    )
    payload = add_edges(payload, key, extra, before, after)
    received = lax.all_to_all(
        payload.reshape(peers, SLOTS, columns + EXTRA),
        "patch",
        split_axis=0,
        concat_axis=0,
        tiled=True,
    ).reshape(peers * SLOTS, columns + EXTRA)
    difference, coefficients = fit(received, science[0])
    return (difference[None], coefficients[None])


def solution(mesh):
    placed = (P("patch", None, "det"), P("patch"), P("patch"), P("patch"), P("patch", None, "det"))
    return jax.shard_map(
        body,
        mesh=mesh,
        in_specs=placed,
        out_specs=(P("patch", None, "det"), P("patch", "det", None)),
        check_vma=False,
    )
```

```python
import jax
import jax.numpy as jnp
import numpy as np
from jax import lax
from jax.experimental import pallas as pl
from jax.experimental.pallas import tpu as pltpu
from jax.sharding import PartitionSpec as P

BASIS = 45
SIGMAS = (0.7, 1.5, 3.0)
RIDGE = 0.01
TAPS = 21
REACH = 10
ROWS = 8
TROWS = 32
SLOTS = 8
EXTRA = 128
SPREAD = 32
ONE = 64
KP = 48
UNKNOWNS = BASIS + 1
VMEM_LIMIT = 12 * 2**20
F32 = jnp.float32
BF16 = jnp.bfloat16


def tap_table():
    offsets = np.arange(TAPS, dtype=np.float64) - REACH
    profiles = []
    for width in SIGMAS:
        for degree in range(5):
            scaled = offsets / width
            profile = scaled**degree * np.exp(-0.5 * scaled * scaled)
            profiles.append(profile / np.sqrt(np.sum(profile * profile)))
    table = np.zeros((ROWS, KP, TAPS, TROWS))
    k = 0
    for s in range(3):
        for i in range(5):
            for j in range(5 - i):
                kernel = np.outer(profiles[5 * s + i], profiles[5 * s + j])
                for o in range(ROWS):
                    table[o, k, :, o : o + TAPS] = kernel
                k += 1
    table = table.reshape(ROWS * KP, TAPS * TROWS).astype(np.float32)
    high = table.astype(BF16)
    low = (table - high.astype(np.float32)).astype(BF16)
    return np.concatenate([high, high, low], axis=1)


def iota(shape, dim):
    return lax.broadcasted_iota(jnp.int32, shape, dim)


def split(x):
    high = x.astype(BF16)
    return high, (x - high.astype(F32)).astype(BF16)


def pick_rows(key, base, step):
    shape = (step, key.shape[1])
    return (iota(shape, 0) + base == key).astype(F32).astype(BF16)


def pack_kernel(strips_ref, notes_ref, out_ref, key_ref, extra_ref):
    count = notes_ref.shape[1]
    patch_row, row_row, weight_row = (notes_ref[i : i + 1, :] for i in range(3))
    lines, columns = strips_ref.shape
    reps = lines // count
    first, second = iota((count, count), 0), iota((count, count), 1)
    patch = jnp.broadcast_to(patch_row, (count, count))
    patch_col = jnp.sum(jnp.where(first == second, patch, 0.0), axis=1, keepdims=True)
    earlier = (patch == patch_col) & (first < second)
    occurrence = jnp.sum(jnp.where(earlier, 1.0, 0.0), axis=0, keepdims=True)
    place = 2.0 * patch_row + occurrence
    spread = (iota((count, lines), 1) // reps == iota((count, lines), 0)).astype(F32).astype(BF16)
    wide = jnp.dot(
        jnp.broadcast_to(place, (8, count)).astype(BF16), spread, preferred_element_type=F32
    )[:1]
    key = wide.astype(jnp.int32) * reps + iota((1, lines), 1) % reps
    key_ref[...] = key
    strips = strips_ref[...]
    step = 256
    for base in range(0, out_ref.shape[0], step):
        out_ref[base : base + step, :] = jnp.dot(
            pick_rows(key, base, step), strips, preferred_element_type=F32
        ).astype(BF16)
    here = iota((lines, count), 0) // reps == iota((lines, count), 1)
    row = jnp.sum(jnp.where(here, row_row, 0.0), axis=1, keepdims=True).astype(jnp.int32)
    weight = jnp.sum(jnp.where(here, weight_row, 0.0), axis=1, keepdims=True)
    lane = iota((lines, EXTRA), 1)
    at = row + iota((lines, EXTRA), 0) % reps + SPREAD
    extra_ref[...] = jnp.where(lane == at, weight, jnp.where(lane == ONE, 1.0, 0.0)).astype(BF16)


def edge_kernel(key_ref, extra_ref, before_ref, after_ref, unused_ref, out_ref):
    lane = iota(extra_ref.shape, 1)
    extra = jnp.where(
        lane < REACH,
        after_ref[...].astype(F32),
        jnp.where(lane >= EXTRA - REACH, before_ref[...].astype(F32), extra_ref[...].astype(F32)),
    ).astype(BF16)
    key = key_ref[...]
    step = 256
    for base in range(0, out_ref.shape[0], step):
        out_ref[base : base + step, :] = jnp.dot(
            pick_rows(key, base, step), extra, preferred_element_type=F32
        ).astype(BF16)


def invert_pair(a, b, d):
    inverse = 1.0 / (a * d - b * b)
    return d * inverse, -b * inverse, a * inverse


def solve_block(m, rows):
    a, b, d = invert_pair(m[0][0], m[0][1], m[1][1])
    first = [a * rows[0] + b * rows[1], b * rows[0] + d * rows[1]]
    if len(rows) == 2:
        return first
    w = [[a * m[0][j] + b * m[1][j] for j in (2, 3)], [b * m[0][j] + d * m[1][j] for j in (2, 3)]]
    s = [[m[2 + i][2 + j] - m[0][2 + i] * w[0][j] - m[1][2 + i] * w[1][j] for j in (0, 1)] for i in (0, 1)]
    a, b, d = invert_pair(s[0][0], s[0][1], s[1][1])
    rest = [rows[2 + i] - m[0][2 + i] * first[0] - m[1][2 + i] * first[1] for i in (0, 1)]
    last = [a * rest[0] + b * rest[1], b * rest[0] + d * rest[1]]
    return [first[i] - w[i][0] * last[0] - w[i][1] * last[1] for i in (0, 1)] + last


def spread_columns(groups, k):
    return [
        [jnp.broadcast_to(g[:, j : j + 1], g.shape) for g in groups]
        for j in range(k, min(k + 4, UNKNOWNS))
    ]


def eliminate(groups, block, spread, own, at, line):
    new = solve_block(block, [groups[own][at + i : at + i + 1] for i in range(len(spread))])
    for column, row in zip(spread, new):
        groups = [g - c * row for g, c in zip(groups, column)]
    for i, row in enumerate(new):
        groups[own] = jnp.where(line == at + i, row, groups[own])
    return groups


def fit_kernel(
    received_ref, science_ref, table_ref,
    difference_ref, coefficients_ref, design_ref, parts_ref,
):
    columns = science_ref.shape[1]
    sums = lax.dot_general(
        received_ref[:, columns:],
        received_ref[...],
        (((0,), (0,)), ((), ())),
        preferred_element_type=F32,
    )[SPREAD : SPREAD + TROWS]
    coverage = sums[:, columns + ONE : columns + ONE + 1]
    template = sums / (1.0 + coverage)
    edges = template[:, columns:]
    upper, lower = split(jnp.concatenate([edges, template[:, :columns], edges], axis=1))
    left = EXTRA - REACH
    upper_taps = jnp.concatenate([upper[:, left + a : left + a + columns] for a in range(TAPS)])
    lower_taps = jnp.concatenate([lower[:, left + a : left + a + columns] for a in range(TAPS)])
    basis = jnp.dot(
        table_ref[...],
        jnp.concatenate([upper_taps, lower_taps, upper_taps]),
        preferred_element_type=F32,
    )
    science = science_ref[...]
    place = iota((8, columns), 0)
    for o in range(ROWS):
        image = basis[o * KP : (o + 1) * KP]
        tail = jnp.where(place == BASIS - KP + 8, 1.0, image[KP - 8 :])
        tail = jnp.where(place == UNKNOWNS - KP + 8, science[o : o + 1], tail)
        image = jnp.concatenate([image[: KP - 8], tail])
        design_ref[o] = image
        image_high, image_low = split(image)
        parts_ref[:KP, o * columns : (o + 1) * columns] = image_high
        parts_ref[KP:, o * columns : (o + 1) * columns] = image_low
    parts = parts_ref[...]
    gram = lax.dot_general(parts, parts, (((1,), (1,)), ((), ())), preferred_element_type=F32)
    half = gram[:KP] + gram[KP:]
    system = half[:, :KP] + half[:, KP:]
    down, across = iota((KP, KP), 0), iota((KP, KP), 1)
    diagonal = (down == across) & (down < UNKNOWNS)
    trace = jnp.sum(jnp.where(diagonal, system, 0.0))
    system = system + jnp.where(diagonal, RIDGE * trace / UNKNOWNS, 0.0)
    groups = [system[g : g + 8] for g in range(0, KP, 8)]
    line = iota((8, KP), 0)
    spread = spread_columns(groups, 0)
    for k in range(0, UNKNOWNS, 4):
        at, own, size = k % 8, k // 8, len(spread)
        ahead = spread_columns(groups, k + 4)
        block = [[c[own][at + i : at + i + 1] for c in spread] for i in range(size)]
        groups = eliminate(groups, block, spread, own, at, line)
        spread = [eliminate(c, block, spread, own, at, line) for c in ahead]
    system = jnp.concatenate(groups)
    fitted = jnp.where(down[:, :1] < UNKNOWNS, system[:, UNKNOWNS : UNKNOWNS + 1], 0.0)
    coefficients_ref[...] = jnp.sum(jnp.where(down == across, fitted, 0.0), axis=0, keepdims=True)[
        :, :UNKNOWNS
    ]
    for o in range(ROWS):
        model = jnp.sum(design_ref[o] * fitted, axis=0, keepdims=True)
        difference_ref[o : o + 1, :] = science[o : o + 1] - model


def call(kernel, outs, *args, **options):
    return pl.pallas_call(
        kernel,
        out_shape=[jax.ShapeDtypeStruct(shape, dtype) for shape, dtype in outs],
        name=kernel.__name__,
        compiler_params=pltpu.CompilerParams(vmem_limit_bytes=VMEM_LIMIT),
        **options,
    )(*args)


def pack(strips, strip_patch, strip_row, strip_weight, peers):
    lines, columns = strips.shape
    notes = jnp.stack([x.astype(F32) for x in (strip_patch, strip_row, strip_weight)])
    return call(
        pack_kernel,
        [
            ((peers * SLOTS, columns + EXTRA), BF16),
            ((1, lines), jnp.int32),
            ((lines, EXTRA), BF16),
        ],
        strips,
        notes,
        grid=(1,),
        out_specs=[
            pl.BlockSpec((peers * SLOTS, columns), lambda i: (0, 0)),
            pl.BlockSpec((1, lines), lambda i: (0, 0)),
            pl.BlockSpec((lines, EXTRA), lambda i: (0, 0)),
        ],
        cost_estimate=pl.CostEstimate(flops=10**9, bytes_accessed=2 * 10**6, transcendentals=0),
    )


def add_edges(payload, key, extra, before, after):
    rows, wide = payload.shape
    lines = key.shape[1]
    block = pl.BlockSpec((rows, EXTRA), lambda i: (0, wide // EXTRA - 1))
    whole = pl.BlockSpec((lines, EXTRA), lambda i: (0, 0))
    (payload,) = call(
        edge_kernel,
        [(payload.shape, BF16)],
        key,
        extra,
        before,
        after,
        payload,
        grid=(1,),
        in_specs=[pl.BlockSpec((1, lines), lambda i: (0, 0)), whole, whole, whole]
        + [pl.BlockSpec(memory_space=pl.ANY)],
        out_specs=[block],
        input_output_aliases={4: 0},
    )
    return payload


def fit(received, science):
    rows, columns = science.shape
    return call(
        fit_kernel,
        [((rows, columns), F32), ((1, UNKNOWNS), F32)],
        received,
        science,
        jnp.asarray(tap_table()),
        scratch_shapes=[
            pltpu.VMEM((ROWS, KP, columns), F32),
            pltpu.VMEM((2 * KP, ROWS * columns), BF16),
        ],
    )


def body(strips, strip_patch, strip_row, strip_weight, science):
    peers = lax.axis_size("patch")
    devices = lax.axis_size("det")
    count, lines, columns = strips.shape
    up = [(i, i + 1) for i in range(devices - 1)]
    down = [(j, i) for i, j in up]
    last = strips[:, :, columns - EXTRA :].reshape(count * lines, EXTRA)
    first = strips[:, :, :EXTRA].reshape(count * lines, EXTRA)
    before = lax.ppermute(last, "det", up)
    after = lax.ppermute(first, "det", down)
    payload, key, extra = pack(
        strips.reshape(count * lines, columns), strip_patch, strip_row, strip_weight, peers
    )
    payload = add_edges(payload, key, extra, before, after)
    received = lax.all_to_all(
        payload.reshape(peers, SLOTS, columns + EXTRA),
        "patch",
        split_axis=0,
        concat_axis=0,
        tiled=True,
    ).reshape(peers * SLOTS, columns + EXTRA)
    difference, coefficients = fit(received, science[0])
    return (difference[None], coefficients[None])


def solution(mesh):
    placed = (P("patch", None, "det"), P("patch"), P("patch"), P("patch"), P("patch", None, "det"))
    return jax.shard_map(
        body,
        mesh=mesh,
        in_specs=placed,
        out_specs=(P("patch", None, "det"), P("patch", "det", None)),
        check_vma=False,
    )
```

```python
import jax
import jax.numpy as jnp
import numpy as np
from jax import lax
from jax.experimental import pallas as pl
from jax.experimental.pallas import tpu as pltpu
from jax.sharding import PartitionSpec as P

BASIS = 45
SIGMAS = (0.7, 1.5, 3.0)
RIDGE = 0.01
TAPS = 21
REACH = 10
ROWS = 8
TROWS = 32
LANES = 128
TILES = 9
NOTES = 4
HALF = 64
EDGE = 32
ONE = 52
TURN = 86
KP = 48
UNKNOWNS = BASIS + 1
VMEM_LIMIT = 12 * 2**20
F32 = jnp.float32
BF16 = jnp.bfloat16


def tap_table():
    offsets = np.arange(TAPS, dtype=np.float64) - REACH
    profiles = []
    for width in SIGMAS:
        for degree in range(5):
            scaled = offsets / width
            profile = scaled**degree * np.exp(-0.5 * scaled * scaled)
            profiles.append(profile / np.sqrt(np.sum(profile * profile)))
    table = np.zeros((ROWS, KP, TAPS, TROWS))
    k = 0
    for s in range(3):
        for i in range(5):
            for j in range(5 - i):
                kernel = np.outer(profiles[5 * s + i], profiles[5 * s + j])
                for o in range(ROWS):
                    table[o, k, :, o : o + TAPS] = kernel
                k += 1
    table = table.reshape(ROWS * KP, TAPS * TROWS).astype(np.float32)
    high = table.astype(BF16)
    low = (table - high.astype(np.float32)).astype(BF16)
    return np.concatenate([high, high, low], axis=1)


def iota(shape, dim):
    return lax.broadcasted_iota(jnp.int32, shape, dim)


def split(x):
    high = x.astype(BF16)
    return high, (x - high.astype(F32)).astype(BF16)


def pick_rows(key, base, step):
    shape = (step, key.shape[1])
    return (iota(shape, 0) + base == key).astype(F32).astype(BF16)


def pack_kernel(strips_ref, about_ref, out_ref, key_ref, notes_ref, second_ref):
    count = about_ref.shape[1]
    patch_row, row_row, weight_row = (about_ref[i : i + 1, :] for i in range(3))
    lines, columns = strips_ref.shape
    reps = lines // count
    first, second = iota((count, count), 0), iota((count, count), 1)
    patch = jnp.broadcast_to(patch_row, (count, count))
    patch_col = jnp.sum(jnp.where(first == second, patch, 0.0), axis=1, keepdims=True)
    earlier = (patch == patch_col) & (first < second)
    slot = jnp.sum(jnp.where(earlier, 1.0, 0.0), axis=0, keepdims=True)
    spread = (iota((count, lines), 1) // reps == iota((count, lines), 0)).astype(F32).astype(BF16)
    wide = jnp.dot(
        jnp.where(iota((8, count), 0) == 0, 2.0 * patch_row + slot, patch_row).astype(BF16),
        spread,
        preferred_element_type=F32,
    ).astype(jnp.int32) * reps + iota((8, lines), 1) % reps
    key = wide[:1]
    key_ref[...] = wide[1:2]
    strips = strips_ref[...]
    step = 256
    pairs = step // 16
    for i in range(out_ref.shape[0] // pairs):
        picked = jnp.dot(pick_rows(key, i * step, step), strips, preferred_element_type=F32)
        picked = picked.reshape(pairs, 2, 8, columns)
        for c in range(columns // LANES):
            for odd in range(2):
                out_ref[i * pairs : (i + 1) * pairs, c + odd * (NOTES + 1)] = picked[
                    :, odd, :, c * LANES : (c + 1) * LANES
                ].astype(BF16)
    here = iota((lines, count), 0) // reps == iota((lines, count), 1)

    def line_of(values):
        return jnp.sum(jnp.where(here, values, 0.0), axis=1, keepdims=True)

    lane = iota((lines, LANES), 1)
    start = line_of(slot).astype(jnp.int32) * HALF
    at = start + line_of(row_row).astype(jnp.int32) + iota((lines, LANES), 0) % reps
    notes_ref[...] = jnp.where(
        lane == at, line_of(weight_row), jnp.where(lane == start + ONE, 1.0, 0.0)
    ).astype(BF16)
    second_ref[...] = jnp.broadcast_to(line_of(slot), (lines, LANES)).astype(BF16)


def notes_kernel(key_ref, notes_ref, second_ref, before_ref, after_ref, unused_ref, out_ref):
    lane = iota(notes_ref.shape, 1)
    edges = jnp.where(
        lane < REACH,
        after_ref[...].astype(F32),
        jnp.where(lane >= LANES - REACH, before_ref[...].astype(F32), 0.0),
    )
    edges = pltpu.roll(edges, LANES - TURN, 1)
    edges = jnp.where(second_ref[...].astype(F32) > 0.5, pltpu.roll(edges, HALF, 1), edges)
    notes = (notes_ref[...].astype(F32) + edges).astype(BF16)
    key = key_ref[...]
    step = 256
    pairs = step // 8
    for i in range(out_ref.shape[0] // pairs):
        picked = jnp.dot(pick_rows(key, i * step, step), notes, preferred_element_type=F32)
        out_ref[i * pairs : (i + 1) * pairs, 0] = picked.reshape(pairs, 8, LANES).astype(BF16)


def invert_pair(a, b, d):
    inverse = 1.0 / (a * d - b * b)
    return d * inverse, -b * inverse, a * inverse


def solve_block(m, rows):
    a, b, d = invert_pair(m[0][0], m[0][1], m[1][1])
    first = [a * rows[0] + b * rows[1], b * rows[0] + d * rows[1]]
    if len(rows) == 2:
        return first
    w = [[a * m[0][j] + b * m[1][j] for j in (2, 3)], [b * m[0][j] + d * m[1][j] for j in (2, 3)]]
    s = [[m[2 + i][2 + j] - m[0][2 + i] * w[0][j] - m[1][2 + i] * w[1][j] for j in (0, 1)] for i in (0, 1)]
    a, b, d = invert_pair(s[0][0], s[0][1], s[1][1])
    rest = [rows[2 + i] - m[0][2 + i] * first[0] - m[1][2 + i] * first[1] for i in (0, 1)]
    last = [a * rest[0] + b * rest[1], b * rest[0] + d * rest[1]]
    return [first[i] - w[i][0] * last[0] - w[i][1] * last[1] for i in (0, 1)] + last


def spread_columns(groups, k):
    return [
        [jnp.broadcast_to(g[:, j : j + 1], g.shape) for g in groups]
        for j in range(k, min(k + 4, UNKNOWNS))
    ]


def eliminate(groups, block, spread, own, at, line):
    new = solve_block(block, [groups[own][at + i : at + i + 1] for i in range(len(spread))])
    for column, row in zip(spread, new):
        groups = [g - c * row for g, c in zip(groups, column)]
    for i, row in enumerate(new):
        groups[own] = jnp.where(line == at + i, row, groups[own])
    return groups


def fit_kernel(
    odd_ref, received_ref, science_ref, table_ref,
    difference_ref, coefficients_ref, design_ref, parts_ref,
):
    columns = science_ref.shape[1]
    odd = odd_ref[0]

    def tile(i):
        return received_ref[:, i].astype(F32)

    low = iota((received_ref.shape[0], 8, LANES), 1) < 4
    whole, off = (NOTES + 1) * odd, NOTES * (1 - odd)
    parts = [
        jnp.concatenate([tile(whole + c), jnp.where(low, tile(off + 1 + c), tile(off + c))])
        for c in range(columns // LANES)
    ]
    mine, other = tile(NOTES), tile(2 * off)
    mine_turned, other_turned = pltpu.roll(mine, 4, 1), pltpu.roll(other, 4, 1)
    mine, mine_turned = (
        jnp.where(odd == 1, mine_turned, mine),
        jnp.where(odd == 1, mine, mine_turned),
    )
    other, other_turned = (
        jnp.where(odd == 1, other_turned, other),
        jnp.where(odd == 1, other, other_turned),
    )
    spread = jnp.concatenate(
        [
            jnp.where(low, mine, pltpu.roll(mine_turned, HALF, 2)),
            jnp.where(low, pltpu.roll(other_turned, HALF, 2), other),
        ]
    )
    lines = 2 * received_ref.shape[0] * 8
    spread = spread.reshape(lines, LANES).astype(BF16)
    strips = jnp.concatenate(
        [x.reshape(lines, LANES).astype(BF16) for x in parts] + [spread], axis=1
    )
    sums = lax.dot_general(
        spread, strips, (((0,), (0,)), ((), ())), preferred_element_type=F32
    )[:TROWS]
    coverage = sums[:, columns + ONE : columns + ONE + 1]
    template = sums / (1.0 + coverage)
    edges = pltpu.roll(template[:, columns:], TURN, 1)
    left = LANES - REACH
    upper, lower = split(jnp.concatenate([edges, template[:, :columns], edges], axis=1))
    upper_taps = jnp.concatenate([upper[:, left + a : left + a + columns] for a in range(TAPS)])
    lower_taps = jnp.concatenate([lower[:, left + a : left + a + columns] for a in range(TAPS)])
    basis = jnp.dot(
        table_ref[...],
        jnp.concatenate([upper_taps, lower_taps, upper_taps]),
        preferred_element_type=F32,
    )
    science = science_ref[...]
    place = iota((8, columns), 0)
    for o in range(ROWS):
        image = basis[o * KP : (o + 1) * KP]
        tail = jnp.where(place == BASIS - KP + 8, 1.0, image[KP - 8 :])
        tail = jnp.where(place == UNKNOWNS - KP + 8, science[o : o + 1], tail)
        image = jnp.concatenate([image[: KP - 8], tail])
        design_ref[o] = image
        image_high, image_low = split(image)
        parts_ref[:KP, o * columns : (o + 1) * columns] = image_high
        parts_ref[KP:, o * columns : (o + 1) * columns] = image_low
    parts = parts_ref[...]
    gram = lax.dot_general(parts, parts, (((1,), (1,)), ((), ())), preferred_element_type=F32)
    half = gram[:KP] + gram[KP:]
    system = half[:, :KP] + half[:, KP:]
    down, across = iota((KP, KP), 0), iota((KP, KP), 1)
    diagonal = (down == across) & (down < UNKNOWNS)
    trace = jnp.sum(jnp.where(diagonal, system, 0.0))
    system = system + jnp.where(diagonal, RIDGE * trace / UNKNOWNS, 0.0)
    groups = [system[g : g + 8] for g in range(0, KP, 8)]
    line = iota((8, KP), 0)
    spread = spread_columns(groups, 0)
    for k in range(0, UNKNOWNS, 4):
        at, own, size = k % 8, k // 8, len(spread)
        ahead = spread_columns(groups, k + 4)
        block = [[c[own][at + i : at + i + 1] for c in spread] for i in range(size)]
        groups = eliminate(groups, block, spread, own, at, line)
        spread = [eliminate(c, block, spread, own, at, line) for c in ahead]
    system = jnp.concatenate(groups)
    fitted = jnp.where(down[:, :1] < UNKNOWNS, system[:, UNKNOWNS : UNKNOWNS + 1], 0.0)
    coefficients_ref[...] = jnp.sum(jnp.where(down == across, fitted, 0.0), axis=0, keepdims=True)[
        :, :UNKNOWNS
    ]
    for o in range(ROWS):
        model = jnp.sum(design_ref[o] * fitted, axis=0, keepdims=True)
        difference_ref[o : o + 1, :] = science[o : o + 1] - model


def call(kernel, outs, *args, **options):
    return pl.pallas_call(
        kernel,
        out_shape=[jax.ShapeDtypeStruct(shape, dtype) for shape, dtype in outs],
        name=kernel.__name__,
        compiler_params=pltpu.CompilerParams(vmem_limit_bytes=VMEM_LIMIT),
        **options,
    )(*args)


def pack(strips, strip_patch, strip_row, strip_weight, peers):
    lines, columns = strips.shape
    about = jnp.stack([x.astype(F32) for x in (strip_patch, strip_row, strip_weight)])
    return call(
        pack_kernel,
        [
            ((peers // 2, TILES, 8, LANES), BF16),
            ((1, lines), jnp.int32),
            ((lines, LANES), BF16),
            ((lines, LANES), BF16),
        ],
        strips,
        about,
        cost_estimate=pl.CostEstimate(flops=10**9, bytes_accessed=2 * 10**6, transcendentals=0),
    )


def add_notes(payload, key, notes, second, before, after):
    pairs = payload.shape[0]
    lines = key.shape[1]
    whole = pl.BlockSpec((lines, LANES), lambda i: (0, 0))
    (payload,) = call(
        notes_kernel,
        [(payload.shape, BF16)],
        key,
        notes,
        second,
        before,
        after,
        payload,
        grid=(1,),
        in_specs=[pl.BlockSpec((1, lines), lambda i: (0, 0)), whole, whole, whole, whole]
        + [pl.BlockSpec(memory_space=pl.ANY)],
        out_specs=[pl.BlockSpec((pairs, 1, 8, LANES), lambda i: (0, NOTES, 0, 0))],
        input_output_aliases={5: 0},
    )
    return payload


def fit(odd, received, science):
    rows, columns = science.shape
    return call(
        fit_kernel,
        [((rows, columns), F32), ((1, UNKNOWNS), F32)],
        odd,
        received,
        science,
        jnp.asarray(tap_table()),
        in_specs=[pl.BlockSpec(memory_space=pltpu.SMEM)]
        + [pl.BlockSpec(memory_space=pltpu.VMEM)] * 3,
        scratch_shapes=[
            pltpu.VMEM((ROWS, KP, columns), F32),
            pltpu.VMEM((2 * KP, ROWS * columns), BF16),
        ],
    )


def body(strips, strip_patch, strip_row, strip_weight, science):
    peers = lax.axis_size("patch")
    devices = lax.axis_size("det")
    count, lines, columns = strips.shape
    up = [(i, i + 1) for i in range(devices - 1)]
    down = [(j, i) for i, j in up]
    last = strips[:, :, columns - LANES :].reshape(count * lines, LANES)
    first = strips[:, :, :LANES].reshape(count * lines, LANES)
    before = lax.ppermute(last, "det", up)
    after = lax.ppermute(first, "det", down)
    payload, *notes = pack(
        strips.reshape(count * lines, columns), strip_patch, strip_row, strip_weight, peers
    )
    odd = (lax.axis_index("patch") & 1).reshape(1)
    payload, odd = lax.optimization_barrier((payload, odd))
    payload = add_notes(payload, *notes, before, after)
    received = lax.all_to_all(
        payload.reshape(peers * TILES, 4, LANES), "patch", split_axis=0, concat_axis=0, tiled=True
    ).reshape(payload.shape)
    difference, coefficients = fit(odd, received, science[0])
    return (difference[None], coefficients[None])


def solution(mesh):
    placed = (P("patch", None, "det"), P("patch"), P("patch"), P("patch"), P("patch", None, "det"))
    return jax.shard_map(
        body,
        mesh=mesh,
        in_specs=placed,
        out_specs=(P("patch", None, "det"), P("patch", "det", None)),
        check_vma=False,
    )
```

```python
import jax
import jax.numpy as jnp
import numpy as np
from jax import lax
from jax.experimental import pallas as pl
from jax.experimental.pallas import tpu as pltpu
from jax.sharding import PartitionSpec as P

BASIS = 45
SIGMAS = (0.7, 1.5, 3.0)
RIDGE = 0.01
TAPS = 21
REACH = 10
ROWS = 8
TROWS = 32
LANES = 128
TILES = 9
NOTES = 4
HALF = 64
BEFORE = 32
AFTER = 48
ONE = 60
KP = 48
UNKNOWNS = BASIS + 1
VMEM_LIMIT = 12 * 2**20
F32 = jnp.float32
BF16 = jnp.bfloat16


def tap_table():
    offsets = np.arange(TAPS, dtype=np.float64) - REACH
    profiles = []
    for width in SIGMAS:
        for degree in range(5):
            scaled = offsets / width
            profile = scaled**degree * np.exp(-0.5 * scaled * scaled)
            profiles.append(profile / np.sqrt(np.sum(profile * profile)))
    table = np.zeros((ROWS, KP, TAPS, TROWS))
    k = 0
    for s in range(3):
        for i in range(5):
            for j in range(5 - i):
                kernel = np.outer(profiles[5 * s + i], profiles[5 * s + j])
                for o in range(ROWS):
                    table[o, k, :, o : o + TAPS] = kernel
                k += 1
    table = table.reshape(ROWS * KP, TAPS * TROWS).astype(np.float32)
    high = table.astype(BF16)
    low = (table - high.astype(np.float32)).astype(BF16)
    return np.concatenate([high, high, low], axis=1)


def iota(shape, dim):
    return lax.broadcasted_iota(jnp.int32, shape, dim)


def split(x):
    high = x.astype(BF16)
    return high, (x - high.astype(F32)).astype(BF16)


def pick_rows(key, base, step):
    shape = (step, key.shape[1])
    return (iota(shape, 0) + base == key).astype(F32).astype(BF16)


def pack_kernel(strips_ref, about_ref, out_ref, key_ref, notes_ref, slot_ref):
    count = about_ref.shape[1]
    patch_row, row_row, weight_row = (about_ref[i : i + 1, :] for i in range(3))
    lines, columns = strips_ref.shape
    reps = lines // count
    first, second = iota((count, count), 0), iota((count, count), 1)
    patch = jnp.broadcast_to(patch_row, (count, count))
    patch_col = jnp.sum(jnp.where(first == second, patch, 0.0), axis=1, keepdims=True)
    earlier = (patch == patch_col) & (first < second)
    slot = jnp.sum(jnp.where(earlier, 1.0, 0.0), axis=0, keepdims=True)
    spread = (iota((count, lines), 1) // reps == iota((count, lines), 0)).astype(F32).astype(BF16)
    facts = jnp.concatenate(
        [2.0 * patch_row + slot, patch_row, row_row, slot, weight_row, jnp.zeros((3, count), F32)]
    )
    wide = jnp.dot(facts.astype(BF16), spread, preferred_element_type=F32)
    line = iota((1, lines), 1) % reps
    key = wide[:1].astype(jnp.int32) * reps + line
    key_ref[...] = wide[1:2].astype(jnp.int32) * reps + line
    slot_ref[...] = wide[3:4]
    start = wide[3:4].astype(jnp.int32) * HALF
    place = iota((LANES, lines), 0)
    notes_ref[...] = jnp.where(
        place == start + wide[2:3].astype(jnp.int32) + line,
        wide[4:5],
        jnp.where(place == start + ONE, 1.0, 0.0),
    ).astype(BF16)
    strips = strips_ref[...]
    step = 256
    pairs = step // 16
    for i in range(out_ref.shape[0] // pairs):
        picked = jnp.dot(pick_rows(key, i * step, step), strips, preferred_element_type=F32)
        picked = picked.reshape(pairs, 2, 8, columns)
        for c in range(columns // LANES):
            for odd in range(2):
                out_ref[i * pairs : (i + 1) * pairs, c + odd * (NOTES + 1)] = picked[
                    :, odd, :, c * LANES : (c + 1) * LANES
                ].astype(BF16)


def notes_kernel(key_ref, notes_ref, slot_ref, before_ref, after_ref, unused_ref, out_ref):
    lines = key_ref.shape[1]

    def padded(edge, rows):
        return [edge.astype(F32), jnp.zeros((rows - REACH, lines), F32)]

    edges = jnp.concatenate(
        [jnp.zeros((BEFORE, lines), F32)]
        + padded(before_ref[...], AFTER - BEFORE)
        + padded(after_ref[...], HALF - AFTER)
    )
    slot = slot_ref[...]
    edges = jnp.concatenate([jnp.where(slot < 0.5, edges, 0.0), jnp.where(slot > 0.5, edges, 0.0)])
    notes = (notes_ref[...].astype(F32) + edges).astype(BF16)
    key = key_ref[...]
    step = 256
    pairs = step // 8
    for i in range(out_ref.shape[0] // pairs):
        picked = lax.dot_general(
            pick_rows(key, i * step, step),
            notes,
            (((1,), (1,)), ((), ())),
            preferred_element_type=F32,
        )
        out_ref[i * pairs : (i + 1) * pairs, 0] = picked.reshape(pairs, 8, LANES).astype(BF16)


def invert_pair(a, b, d):
    inverse = 1.0 / (a * d - b * b)
    return d * inverse, -b * inverse, a * inverse


def solve_block(m, rows):
    a, b, d = invert_pair(m[0][0], m[0][1], m[1][1])
    first = [a * rows[0] + b * rows[1], b * rows[0] + d * rows[1]]
    if len(rows) == 2:
        return first
    w = [[a * m[0][j] + b * m[1][j] for j in (2, 3)], [b * m[0][j] + d * m[1][j] for j in (2, 3)]]
    s = [[m[2 + i][2 + j] - m[0][2 + i] * w[0][j] - m[1][2 + i] * w[1][j] for j in (0, 1)] for i in (0, 1)]
    a, b, d = invert_pair(s[0][0], s[0][1], s[1][1])
    rest = [rows[2 + i] - m[0][2 + i] * first[0] - m[1][2 + i] * first[1] for i in (0, 1)]
    last = [a * rest[0] + b * rest[1], b * rest[0] + d * rest[1]]
    return [first[i] - w[i][0] * last[0] - w[i][1] * last[1] for i in (0, 1)] + last


def spread_columns(groups, k):
    return [
        [jnp.broadcast_to(g[:, j : j + 1], g.shape) for g in groups]
        for j in range(k, min(k + 4, UNKNOWNS))
    ]


def eliminate(groups, block, spread, own, at, line):
    new = solve_block(block, [groups[own][at + i : at + i + 1] for i in range(len(spread))])
    for column, row in zip(spread, new):
        groups = [g - c * row for g, c in zip(groups, column)]
    for i, row in enumerate(new):
        groups[own] = jnp.where(line == at + i, row, groups[own])
    return groups


def fit_kernel(
    odd_ref, received_ref, science_ref, table_ref,
    difference_ref, coefficients_ref, design_ref, parts_ref,
):
    columns = science_ref.shape[1]
    odd = odd_ref[0]

    def tile(i):
        return received_ref[:, i].astype(F32)

    low = iota((received_ref.shape[0], 8, LANES), 1) < 4
    whole, off = (NOTES + 1) * odd, NOTES * (1 - odd)
    parts = [
        jnp.concatenate([tile(whole + c), jnp.where(low, tile(off + 1 + c), tile(off + c))])
        for c in range(columns // LANES)
    ]
    mine, other = tile(NOTES), tile(2 * off)
    mine_turned, other_turned = pltpu.roll(mine, 4, 1), pltpu.roll(other, 4, 1)
    mine, mine_turned = (
        jnp.where(odd == 1, mine_turned, mine),
        jnp.where(odd == 1, mine, mine_turned),
    )
    other, other_turned = (
        jnp.where(odd == 1, other_turned, other),
        jnp.where(odd == 1, other, other_turned),
    )
    spread = jnp.concatenate(
        [
            jnp.where(low, mine, pltpu.roll(mine_turned, HALF, 2)),
            jnp.where(low, pltpu.roll(other_turned, HALF, 2), other),
        ]
    )
    lines = 2 * received_ref.shape[0] * 8
    spread = spread.reshape(lines, LANES).astype(BF16)
    strips = jnp.concatenate(
        [x.reshape(lines, LANES).astype(BF16) for x in parts] + [spread], axis=1
    )
    sums = lax.dot_general(
        spread, strips, (((0,), (0,)), ((), ())), preferred_element_type=F32
    )[:TROWS]
    coverage = sums[:, columns + ONE : columns + ONE + 1]
    template = sums / (1.0 + coverage)
    edges = template[:, columns:]
    edges = (pltpu.roll(edges, LANES - REACH - BEFORE, 1), pltpu.roll(edges, LANES - AFTER, 1))
    left = LANES - REACH
    upper, lower = split(jnp.concatenate([edges[0], template[:, :columns], edges[1]], axis=1))
    upper_taps = jnp.concatenate([upper[:, left + a : left + a + columns] for a in range(TAPS)])
    lower_taps = jnp.concatenate([lower[:, left + a : left + a + columns] for a in range(TAPS)])
    basis = jnp.dot(
        table_ref[...],
        jnp.concatenate([upper_taps, lower_taps, upper_taps]),
        preferred_element_type=F32,
    )
    science = science_ref[...]
    place = iota((8, columns), 0)
    for o in range(ROWS):
        image = basis[o * KP : (o + 1) * KP]
        tail = jnp.where(place == BASIS - KP + 8, 1.0, image[KP - 8 :])
        tail = jnp.where(place == UNKNOWNS - KP + 8, science[o : o + 1], tail)
        image = jnp.concatenate([image[: KP - 8], tail])
        design_ref[o] = image
        image_high, image_low = split(image)
        parts_ref[:KP, o * columns : (o + 1) * columns] = image_high
        parts_ref[KP:, o * columns : (o + 1) * columns] = image_low
    parts = parts_ref[...]
    gram = lax.dot_general(parts, parts, (((1,), (1,)), ((), ())), preferred_element_type=F32)
    half = gram[:KP] + gram[KP:]
    system = half[:, :KP] + half[:, KP:]
    down, across = iota((KP, KP), 0), iota((KP, KP), 1)
    diagonal = (down == across) & (down < UNKNOWNS)
    trace = jnp.sum(jnp.where(diagonal, system, 0.0))
    system = system + jnp.where(diagonal, RIDGE * trace / UNKNOWNS, 0.0)
    groups = [system[g : g + 8] for g in range(0, KP, 8)]
    line = iota((8, KP), 0)
    spread = spread_columns(groups, 0)
    for k in range(0, UNKNOWNS, 4):
        at, own, size = k % 8, k // 8, len(spread)
        ahead = spread_columns(groups, k + 4)
        block = [[c[own][at + i : at + i + 1] for c in spread] for i in range(size)]
        groups = eliminate(groups, block, spread, own, at, line)
        spread = [eliminate(c, block, spread, own, at, line) for c in ahead]
    system = jnp.concatenate(groups)
    fitted = jnp.where(down[:, :1] < UNKNOWNS, system[:, UNKNOWNS : UNKNOWNS + 1], 0.0)
    coefficients_ref[...] = jnp.sum(jnp.where(down == across, fitted, 0.0), axis=0, keepdims=True)[
        :, :UNKNOWNS
    ]
    for o in range(ROWS):
        model = jnp.sum(design_ref[o] * fitted, axis=0, keepdims=True)
        difference_ref[o : o + 1, :] = science[o : o + 1] - model


def call(kernel, outs, *args, **options):
    return pl.pallas_call(
        kernel,
        out_shape=[jax.ShapeDtypeStruct(shape, dtype) for shape, dtype in outs],
        name=kernel.__name__,
        compiler_params=pltpu.CompilerParams(vmem_limit_bytes=VMEM_LIMIT),
        **options,
    )(*args)


def pack(strips, strip_patch, strip_row, strip_weight, peers):
    lines, columns = strips.shape
    about = jnp.stack([x.astype(F32) for x in (strip_patch, strip_row, strip_weight)])
    return call(
        pack_kernel,
        [
            ((peers // 2, TILES, 8, LANES), BF16),
            ((1, lines), jnp.int32),
            ((LANES, lines), BF16),
            ((1, lines), F32),
        ],
        strips,
        about,
        cost_estimate=pl.CostEstimate(flops=10**9, bytes_accessed=2 * 10**6, transcendentals=0),
    )


def add_notes(payload, *parts):
    (payload,) = call(
        notes_kernel,
        [(payload.shape, BF16)],
        *parts,
        payload,
        grid=(1,),
        in_specs=[pl.BlockSpec(x.shape, lambda i: (0, 0)) for x in parts]
        + [pl.BlockSpec(memory_space=pl.ANY)],
        out_specs=[pl.BlockSpec((payload.shape[0], 1, 8, LANES), lambda i: (0, NOTES, 0, 0))],
        input_output_aliases={len(parts): 0},
    )
    return payload


def fit(odd, received, science):
    rows, columns = science.shape
    return call(
        fit_kernel,
        [((rows, columns), F32), ((1, UNKNOWNS), F32)],
        odd,
        received,
        science,
        jnp.asarray(tap_table()),
        in_specs=[pl.BlockSpec(memory_space=pltpu.SMEM)]
        + [pl.BlockSpec(memory_space=pltpu.VMEM)] * 3,
        scratch_shapes=[
            pltpu.VMEM((ROWS, KP, columns), F32),
            pltpu.VMEM((2 * KP, ROWS * columns), BF16),
        ],
    )


def body(strips, strip_patch, strip_row, strip_weight, science):
    peers = lax.axis_size("patch")
    devices = lax.axis_size("det")
    count, lines, columns = strips.shape
    up = [(i, i + 1) for i in range(devices - 1)]
    down = [(j, i) for i, j in up]
    last = strips[:, :, columns - REACH :].reshape(count * lines, REACH).T
    first = strips[:, :, :REACH].reshape(count * lines, REACH).T
    before = lax.ppermute(last, "det", up)
    after = lax.ppermute(first, "det", down)
    payload, *notes = pack(
        strips.reshape(count * lines, columns), strip_patch, strip_row, strip_weight, peers
    )
    odd = (lax.axis_index("patch") & 1).reshape(1)
    payload, odd = lax.optimization_barrier((payload, odd))
    payload = add_notes(payload, *notes, before, after)
    received = lax.all_to_all(
        payload.reshape(peers * TILES, 4, LANES), "patch", split_axis=0, concat_axis=0, tiled=True
    ).reshape(payload.shape)
    difference, coefficients = fit(odd, received, science[0])
    return (difference[None], coefficients[None])


def solution(mesh):
    placed = (P("patch", None, "det"), P("patch"), P("patch"), P("patch"), P("patch", None, "det"))
    return jax.shard_map(
        body,
        mesh=mesh,
        in_specs=placed,
        out_specs=(P("patch", None, "det"), P("patch", "det", None)),
        check_vma=False,
    )
```

```python
import jax
import jax.numpy as jnp
import numpy as np
from jax import lax
from jax.experimental import pallas as pl
from jax.experimental.pallas import tpu as pltpu
from jax.sharding import PartitionSpec as P

BASIS = 45
SIGMAS = (0.7, 1.5, 3.0)
RIDGE = 0.01
TAPS = 21
REACH = 10
ROWS = 8
TROWS = 32
LANES = 128
TILES = 9
NOTES = 4
HALF = 64
BEFORE = 32
AFTER = 48
ONE = 60
KP = 48
UNKNOWNS = BASIS + 1
VMEM_LIMIT = 12 * 2**20
F32 = jnp.float32
BF16 = jnp.bfloat16


def tap_table():
    offsets = np.arange(TAPS, dtype=np.float64) - REACH
    profiles = []
    for width in SIGMAS:
        for degree in range(5):
            scaled = offsets / width
            profile = scaled**degree * np.exp(-0.5 * scaled * scaled)
            profiles.append(profile / np.sqrt(np.sum(profile * profile)))
    table = np.zeros((ROWS, KP, TAPS, TROWS))
    k = 0
    for s in range(3):
        for i in range(5):
            for j in range(5 - i):
                kernel = np.outer(profiles[5 * s + i], profiles[5 * s + j])
                for o in range(ROWS):
                    table[o, k, :, o : o + TAPS] = kernel
                k += 1
    table = table.reshape(ROWS * KP, TAPS * TROWS).astype(np.float32)
    high = table.astype(BF16)
    low = (table - high.astype(np.float32)).astype(BF16)
    return np.concatenate([high, low])


def iota(shape, dim):
    return lax.broadcasted_iota(jnp.int32, shape, dim)


def split(x):
    high = x.astype(BF16)
    return high, (x - high.astype(F32)).astype(BF16)


def pick_rows(key, base, step):
    shape = (step, key.shape[1])
    return (iota(shape, 0) + base == key).astype(F32).astype(BF16)


def pack_kernel(strips_ref, about_ref, out_ref, key_ref, notes_ref, slot_ref):
    count = about_ref.shape[1]
    patch_row, row_row, weight_row = (about_ref[i : i + 1, :] for i in range(3))
    lines, columns = strips_ref.shape
    reps = lines // count
    first, second = iota((count, count), 0), iota((count, count), 1)
    patch = jnp.broadcast_to(patch_row, (count, count))
    patch_col = jnp.sum(jnp.where(first == second, patch, 0.0), axis=1, keepdims=True)
    earlier = (patch == patch_col) & (first < second)
    slot = jnp.sum(jnp.where(earlier, 1.0, 0.0), axis=0, keepdims=True)
    spread = (iota((count, lines), 1) // reps == iota((count, lines), 0)).astype(F32).astype(BF16)
    facts = jnp.concatenate(
        [2.0 * patch_row + slot, patch_row, row_row, slot, weight_row, jnp.zeros((3, count), F32)]
    )
    wide = jnp.dot(facts.astype(BF16), spread, preferred_element_type=F32)
    line = iota((1, lines), 1) % reps
    key = wide[:1].astype(jnp.int32) * reps + line
    key_ref[...] = wide[1:2].astype(jnp.int32) * reps + line
    slot_ref[...] = wide[3:4]
    start = wide[3:4].astype(jnp.int32) * HALF
    place = iota((LANES, lines), 0)
    notes_ref[...] = jnp.where(
        place == start + wide[2:3].astype(jnp.int32) + line,
        wide[4:5],
        jnp.where(place == start + ONE, 1.0, 0.0),
    ).astype(BF16)
    strips = strips_ref[...]
    step = 256
    pairs = step // 16
    for i in range(out_ref.shape[0] // pairs):
        picked = jnp.dot(pick_rows(key, i * step, step), strips, preferred_element_type=F32)
        picked = picked.reshape(pairs, 2, 8, columns)
        for c in range(columns // LANES):
            for odd in range(2):
                out_ref[i * pairs : (i + 1) * pairs, c + odd * (NOTES + 1)] = picked[
                    :, odd, :, c * LANES : (c + 1) * LANES
                ].astype(BF16)


def notes_kernel(key_ref, notes_ref, slot_ref, before_ref, after_ref, unused_ref, out_ref):
    lines = key_ref.shape[1]

    def padded(edge, rows):
        return [edge.astype(F32), jnp.zeros((rows - REACH, lines), F32)]

    edges = jnp.concatenate(
        [jnp.zeros((BEFORE, lines), F32)]
        + padded(before_ref[...], AFTER - BEFORE)
        + padded(after_ref[...], HALF - AFTER)
    )
    slot = slot_ref[...]
    edges = jnp.concatenate([jnp.where(slot < 0.5, edges, 0.0), jnp.where(slot > 0.5, edges, 0.0)])
    notes = (notes_ref[...].astype(F32) + edges).astype(BF16)
    key = key_ref[...]
    step = 256
    pairs = step // 8
    for i in range(out_ref.shape[0] // pairs):
        picked = lax.dot_general(
            pick_rows(key, i * step, step),
            notes,
            (((1,), (1,)), ((), ())),
            preferred_element_type=F32,
        )
        out_ref[i * pairs : (i + 1) * pairs, 0] = picked.reshape(pairs, 8, LANES).astype(BF16)


def invert_pair(a, b, d):
    inverse = 1.0 / (a * d - b * b)
    return d * inverse, -b * inverse, a * inverse


def solve_block(m, rows):
    a, b, d = invert_pair(m[0][0], m[0][1], m[1][1])
    first = [a * rows[0] + b * rows[1], b * rows[0] + d * rows[1]]
    if len(rows) == 2:
        return first
    w = [[a * m[0][j] + b * m[1][j] for j in (2, 3)], [b * m[0][j] + d * m[1][j] for j in (2, 3)]]
    s = [[m[2 + i][2 + j] - m[0][2 + i] * w[0][j] - m[1][2 + i] * w[1][j] for j in (0, 1)] for i in (0, 1)]
    a, b, d = invert_pair(s[0][0], s[0][1], s[1][1])
    rest = [rows[2 + i] - m[0][2 + i] * first[0] - m[1][2 + i] * first[1] for i in (0, 1)]
    last = [a * rest[0] + b * rest[1], b * rest[0] + d * rest[1]]
    return [first[i] - w[i][0] * last[0] - w[i][1] * last[1] for i in (0, 1)] + last


def spread_columns(groups, k):
    return [
        [jnp.broadcast_to(g[:, j : j + 1], g.shape) for g in groups]
        for j in range(k, min(k + 4, UNKNOWNS))
    ]


def eliminate(groups, block, spread, own, at, line):
    new = solve_block(block, [groups[own][at + i : at + i + 1] for i in range(len(spread))])
    for column, row in zip(spread, new):
        groups = [g - c * row for g, c in zip(groups, column)]
    for i, row in enumerate(new):
        groups[own] = jnp.where(line == at + i, row, groups[own])
    return groups


def fit_kernel(
    odd_ref, received_ref, science_ref, table_ref,
    difference_ref, coefficients_ref, design_ref, parts_ref,
):
    columns = science_ref.shape[1]
    odd = odd_ref[0]

    def tile(i):
        return received_ref[:, i].astype(F32)

    low = iota((received_ref.shape[0], 8, LANES), 1) < 4
    whole, off = (NOTES + 1) * odd, NOTES * (1 - odd)
    parts = [
        jnp.concatenate([tile(whole + c), jnp.where(low, tile(off + 1 + c), tile(off + c))])
        for c in range(columns // LANES)
    ]
    mine, other = tile(NOTES), tile(2 * off)
    mine_turned, other_turned = pltpu.roll(mine, 4, 1), pltpu.roll(other, 4, 1)
    mine, mine_turned = (
        jnp.where(odd == 1, mine_turned, mine),
        jnp.where(odd == 1, mine, mine_turned),
    )
    other, other_turned = (
        jnp.where(odd == 1, other_turned, other),
        jnp.where(odd == 1, other, other_turned),
    )
    spread = jnp.concatenate(
        [
            jnp.where(low, mine, pltpu.roll(mine_turned, HALF, 2)),
            jnp.where(low, pltpu.roll(other_turned, HALF, 2), other),
        ]
    )
    lines = 2 * received_ref.shape[0] * 8
    spread = spread.reshape(lines, LANES).astype(BF16)
    strips = jnp.concatenate(
        [x.reshape(lines, LANES).astype(BF16) for x in parts] + [spread], axis=1
    )
    sums = lax.dot_general(
        spread, strips, (((0,), (0,)), ((), ())), preferred_element_type=F32
    )[:TROWS]
    coverage = sums[:, columns + ONE : columns + ONE + 1]
    template = sums / (1.0 + coverage)
    edges = template[:, columns:]
    edges = (pltpu.roll(edges, LANES - REACH - BEFORE, 1), pltpu.roll(edges, LANES - AFTER, 1))
    left = LANES - REACH
    upper, lower = split(jnp.concatenate([edges[0], template[:, :columns], edges[1]], axis=1))
    upper_taps = jnp.concatenate([upper[:, left + a : left + a + columns] for a in range(TAPS)])
    lower_taps = jnp.concatenate([lower[:, left + a : left + a + columns] for a in range(TAPS)])
    tall = jnp.dot(table_ref[...], upper_taps, preferred_element_type=F32)
    basis = tall[: ROWS * KP] + (
        tall[ROWS * KP :]
        + jnp.dot(table_ref[: ROWS * KP], lower_taps, preferred_element_type=F32)
    )
    science = science_ref[...]
    place = iota((8, columns), 0)
    for o in range(ROWS):
        image = basis[o * KP : (o + 1) * KP]
        tail = jnp.where(place == BASIS - KP + 8, 1.0, image[KP - 8 :])
        tail = jnp.where(place == UNKNOWNS - KP + 8, science[o : o + 1], tail)
        image = jnp.concatenate([image[: KP - 8], tail])
        design_ref[o] = image
        image_high, image_low = split(image)
        parts_ref[:KP, o * columns : (o + 1) * columns] = image_high
        parts_ref[KP:, o * columns : (o + 1) * columns] = image_low
    parts = parts_ref[...]
    gram = lax.dot_general(parts, parts, (((1,), (1,)), ((), ())), preferred_element_type=F32)
    half = gram[:KP] + gram[KP:]
    system = half[:, :KP] + half[:, KP:]
    down, across = iota((KP, KP), 0), iota((KP, KP), 1)
    diagonal = (down == across) & (down < UNKNOWNS)
    trace = jnp.sum(jnp.where(diagonal, system, 0.0))
    system = system + jnp.where(diagonal, RIDGE * trace / UNKNOWNS, 0.0)
    groups = [system[g : g + 8] for g in range(0, KP, 8)]
    line = iota((8, KP), 0)
    spread = spread_columns(groups, 0)
    for k in range(0, UNKNOWNS, 4):
        at, own, size = k % 8, k // 8, len(spread)
        ahead = spread_columns(groups, k + 4)
        block = [[c[own][at + i : at + i + 1] for c in spread] for i in range(size)]
        groups = eliminate(groups, block, spread, own, at, line)
        spread = [eliminate(c, block, spread, own, at, line) for c in ahead]
    system = jnp.concatenate(groups)
    fitted = jnp.where(down[:, :1] < UNKNOWNS, system[:, UNKNOWNS : UNKNOWNS + 1], 0.0)
    coefficients_ref[...] = jnp.sum(jnp.where(down == across, fitted, 0.0), axis=0, keepdims=True)[
        :, :UNKNOWNS
    ]
    for o in range(ROWS):
        model = jnp.sum(design_ref[o] * fitted, axis=0, keepdims=True)
        difference_ref[o : o + 1, :] = science[o : o + 1] - model


def call(kernel, outs, *args, **options):
    return pl.pallas_call(
        kernel,
        out_shape=[jax.ShapeDtypeStruct(shape, dtype) for shape, dtype in outs],
        name=kernel.__name__,
        compiler_params=pltpu.CompilerParams(vmem_limit_bytes=VMEM_LIMIT),
        **options,
    )(*args)


def pack(strips, strip_patch, strip_row, strip_weight, peers):
    lines, columns = strips.shape
    about = jnp.stack([x.astype(F32) for x in (strip_patch, strip_row, strip_weight)])
    return call(
        pack_kernel,
        [
            ((peers // 2, TILES, 8, LANES), BF16),
            ((1, lines), jnp.int32),
            ((LANES, lines), BF16),
            ((1, lines), F32),
        ],
        strips,
        about,
        cost_estimate=pl.CostEstimate(flops=10**9, bytes_accessed=2 * 10**6, transcendentals=0),
    )


def add_notes(payload, *parts):
    (payload,) = call(
        notes_kernel,
        [(payload.shape, BF16)],
        *parts,
        payload,
        grid=(1,),
        in_specs=[pl.BlockSpec(x.shape, lambda i: (0, 0)) for x in parts]
        + [pl.BlockSpec(memory_space=pl.ANY)],
        out_specs=[pl.BlockSpec((payload.shape[0], 1, 8, LANES), lambda i: (0, NOTES, 0, 0))],
        input_output_aliases={len(parts): 0},
    )
    return payload


def fit(odd, received, science):
    rows, columns = science.shape
    return call(
        fit_kernel,
        [((rows, columns), F32), ((1, UNKNOWNS), F32)],
        odd,
        received,
        science,
        jnp.asarray(tap_table()),
        in_specs=[pl.BlockSpec(memory_space=pltpu.SMEM)]
        + [pl.BlockSpec(memory_space=pltpu.VMEM)] * 3,
        scratch_shapes=[
            pltpu.VMEM((ROWS, KP, columns), F32),
            pltpu.VMEM((2 * KP, ROWS * columns), BF16),
        ],
    )


def body(strips, strip_patch, strip_row, strip_weight, science):
    peers = lax.axis_size("patch")
    devices = lax.axis_size("det")
    count, lines, columns = strips.shape
    up = [(i, i + 1) for i in range(devices - 1)]
    down = [(j, i) for i, j in up]
    last = strips[:, :, columns - REACH :].reshape(count * lines, REACH).T
    first = strips[:, :, :REACH].reshape(count * lines, REACH).T
    before = lax.ppermute(last, "det", up)
    after = lax.ppermute(first, "det", down)
    payload, *notes = pack(
        strips.reshape(count * lines, columns), strip_patch, strip_row, strip_weight, peers
    )
    odd = (lax.axis_index("patch") & 1).reshape(1)
    payload, odd = lax.optimization_barrier((payload, odd))
    payload = add_notes(payload, *notes, before, after)
    received = lax.all_to_all(
        payload.reshape(peers * TILES, 4, LANES), "patch", split_axis=0, concat_axis=0, tiled=True
    ).reshape(payload.shape)
    difference, coefficients = fit(odd, received, science[0])
    return (difference[None], coefficients[None])


def solution(mesh):
    placed = (P("patch", None, "det"), P("patch"), P("patch"), P("patch"), P("patch", None, "det"))
    return jax.shard_map(
        body,
        mesh=mesh,
        in_specs=placed,
        out_specs=(P("patch", None, "det"), P("patch", "det", None)),
        check_vma=False,
    )
```

```python
import jax
import jax.numpy as jnp
import numpy as np
from jax import lax
from jax.experimental import pallas as pl
from jax.experimental.pallas import tpu as pltpu
from jax.sharding import PartitionSpec as P

BASIS = 45
SIGMAS = (0.7, 1.5, 3.0)
RIDGE = 0.01
TAPS = 21
REACH = 10
ROWS = 8
TROWS = 32
LANES = 128
TILES = 9
NOTES = 4
HALF = 64
BEFORE = 32
AFTER = 48
ONE = 60
KP = 48
UNKNOWNS = BASIS + 1
VMEM_LIMIT = 12 * 2**20
F32 = jnp.float32
BF16 = jnp.bfloat16


def tap_table():
    offsets = np.arange(TAPS, dtype=np.float64) - REACH
    profiles = []
    for width in SIGMAS:
        for degree in range(5):
            scaled = offsets / width
            profile = scaled**degree * np.exp(-0.5 * scaled * scaled)
            profiles.append(profile / np.sqrt(np.sum(profile * profile)))
    table = np.zeros((ROWS, KP, TAPS, TROWS))
    k = 0
    for s in range(3):
        for i in range(5):
            for j in range(5 - i):
                kernel = np.outer(profiles[5 * s + i], profiles[5 * s + j])
                for o in range(ROWS):
                    table[o, k, :, o : o + TAPS] = kernel
                k += 1
    table = table.reshape(ROWS * KP, TAPS * TROWS).astype(np.float32)
    high = table.astype(BF16)
    low = (table - high.astype(np.float32)).astype(BF16)
    return np.concatenate([high, low])


def iota(shape, dim):
    return lax.broadcasted_iota(jnp.int32, shape, dim)


def split(x):
    high = x.astype(BF16)
    return high, (x - high.astype(F32)).astype(BF16)


def pick_rows(key, base, step):
    shape = (step, key.shape[1])
    return (iota(shape, 0) + base == key).astype(F32).astype(BF16)


def pack_kernel(strips_ref, about_ref, out_ref, key_ref, notes_ref, slot_ref):
    count = about_ref.shape[1]
    patch_row, row_row, weight_row = (about_ref[i : i + 1, :] for i in range(3))
    lines, columns = strips_ref.shape
    reps = lines // count
    first, second = iota((count, count), 0), iota((count, count), 1)
    patch = jnp.broadcast_to(patch_row, (count, count))
    patch_col = jnp.sum(jnp.where(first == second, patch, 0.0), axis=1, keepdims=True)
    earlier = (patch == patch_col) & (first < second)
    slot = jnp.sum(jnp.where(earlier, 1.0, 0.0), axis=0, keepdims=True)
    spread = (iota((count, lines), 1) // reps == iota((count, lines), 0)).astype(F32).astype(BF16)
    facts = jnp.concatenate(
        [2.0 * patch_row + slot, patch_row, row_row, slot, weight_row, jnp.zeros((3, count), F32)]
    )
    wide = jnp.dot(facts.astype(BF16), spread, preferred_element_type=F32)
    line = iota((1, lines), 1) % reps
    key = wide[:1].astype(jnp.int32) * reps + line
    key_ref[...] = wide[1:2].astype(jnp.int32) * reps + line
    slot_ref[...] = wide[3:4]
    start = wide[3:4].astype(jnp.int32) * HALF
    place = iota((LANES, lines), 0)
    notes_ref[...] = jnp.where(
        place == start + wide[2:3].astype(jnp.int32) + line,
        wide[4:5],
        jnp.where(place == start + ONE, 1.0, 0.0),
    ).astype(BF16)
    strips = strips_ref[...]
    step = 256
    pairs = step // 16
    for i in range(out_ref.shape[0] // pairs):
        picked = jnp.dot(pick_rows(key, i * step, step), strips, preferred_element_type=F32)
        picked = picked.reshape(pairs, 2, 8, columns)
        for c in range(columns // LANES):
            for odd in range(2):
                out_ref[i * pairs : (i + 1) * pairs, c + odd * (NOTES + 1)] = picked[
                    :, odd, :, c * LANES : (c + 1) * LANES
                ].astype(BF16)


def notes_kernel(key_ref, notes_ref, slot_ref, before_ref, after_ref, unused_ref, out_ref):
    lines = key_ref.shape[1]

    def padded(edge, rows):
        return [edge.astype(F32), jnp.zeros((rows - REACH, lines), F32)]

    edges = jnp.concatenate(
        [jnp.zeros((BEFORE, lines), F32)]
        + padded(before_ref[...], AFTER - BEFORE)
        + padded(after_ref[...], HALF - AFTER)
    )
    slot = slot_ref[...]
    edges = jnp.concatenate([jnp.where(slot < 0.5, edges, 0.0), jnp.where(slot > 0.5, edges, 0.0)])
    notes = (notes_ref[...].astype(F32) + edges).astype(BF16)
    rows = out_ref.shape[0] * 8
    picked = lax.dot_general(
        pick_rows(key_ref[...], 0, rows), notes, (((1,), (1,)), ((), ())), preferred_element_type=F32
    )
    out_ref[:, 0] = picked.reshape(out_ref.shape[0], 8, LANES).astype(BF16)


def invert_pair(a, b, d):
    inverse = 1.0 / (a * d - b * b)
    return d * inverse, -b * inverse, a * inverse


def solve_block(m, rows):
    a, b, d = invert_pair(m[0][0], m[0][1], m[1][1])
    first = [a * rows[0] + b * rows[1], b * rows[0] + d * rows[1]]
    if len(rows) == 2:
        return first
    w = [[a * m[0][j] + b * m[1][j] for j in (2, 3)], [b * m[0][j] + d * m[1][j] for j in (2, 3)]]
    s = [[m[2 + i][2 + j] - m[0][2 + i] * w[0][j] - m[1][2 + i] * w[1][j] for j in (0, 1)] for i in (0, 1)]
    a, b, d = invert_pair(s[0][0], s[0][1], s[1][1])
    rest = [rows[2 + i] - m[0][2 + i] * first[0] - m[1][2 + i] * first[1] for i in (0, 1)]
    last = [a * rest[0] + b * rest[1], b * rest[0] + d * rest[1]]
    return [first[i] - w[i][0] * last[0] - w[i][1] * last[1] for i in (0, 1)] + last


def spread_columns(groups, k):
    return [
        [jnp.broadcast_to(g[:, j : j + 1], g.shape) for g in groups]
        for j in range(k, min(k + 4, UNKNOWNS))
    ]


def eliminate(groups, block, spread, own, at, line):
    new = solve_block(block, [groups[own][at + i : at + i + 1] for i in range(len(spread))])
    for column, row in zip(spread, new):
        groups = [g - c * row for g, c in zip(groups, column)]
    for i, row in enumerate(new):
        groups[own] = jnp.where(line == at + i, row, groups[own])
    return groups


def fit_kernel(
    odd_ref, received_ref, science_ref, table_ref,
    difference_ref, coefficients_ref, design_ref, parts_ref,
):
    columns = science_ref.shape[1]
    odd = odd_ref[0]

    def tile(i):
        return received_ref[:, i].astype(F32)

    low = iota((received_ref.shape[0], 8, LANES), 1) < 4
    whole, off = (NOTES + 1) * odd, NOTES * (1 - odd)
    parts = [
        jnp.concatenate([tile(whole + c), jnp.where(low, tile(off + 1 + c), tile(off + c))])
        for c in range(columns // LANES)
    ]
    mine, other = tile(NOTES), tile(2 * off)
    mine_turned, other_turned = pltpu.roll(mine, 4, 1), pltpu.roll(other, 4, 1)
    mine, mine_turned = (
        jnp.where(odd == 1, mine_turned, mine),
        jnp.where(odd == 1, mine, mine_turned),
    )
    other, other_turned = (
        jnp.where(odd == 1, other_turned, other),
        jnp.where(odd == 1, other, other_turned),
    )
    spread = jnp.concatenate(
        [
            jnp.where(low, mine, pltpu.roll(mine_turned, HALF, 2)),
            jnp.where(low, pltpu.roll(other_turned, HALF, 2), other),
        ]
    )
    lines = 2 * received_ref.shape[0] * 8
    spread = spread.reshape(lines, LANES).astype(BF16)
    strips = jnp.concatenate(
        [x.reshape(lines, LANES).astype(BF16) for x in parts] + [spread], axis=1
    )
    sums = lax.dot_general(
        spread, strips, (((0,), (0,)), ((), ())), preferred_element_type=F32
    )[:TROWS]
    coverage = sums[:, columns + ONE : columns + ONE + 1]
    template = sums / (1.0 + coverage)
    edges = template[:, columns:]
    edges = (pltpu.roll(edges, LANES - REACH - BEFORE, 1), pltpu.roll(edges, LANES - AFTER, 1))
    left = LANES - REACH
    upper, lower = split(jnp.concatenate([edges[0], template[:, :columns], edges[1]], axis=1))
    upper_taps = jnp.concatenate([upper[:, left + a : left + a + columns] for a in range(TAPS)])
    lower_taps = jnp.concatenate([lower[:, left + a : left + a + columns] for a in range(TAPS)])
    tall = jnp.dot(table_ref[...], upper_taps, preferred_element_type=F32)
    basis = tall[: ROWS * KP] + (
        tall[ROWS * KP :]
        + jnp.dot(table_ref[: ROWS * KP], lower_taps, preferred_element_type=F32)
    )
    science = science_ref[...]
    place = iota((8, columns), 0)
    for o in range(ROWS):
        image = basis[o * KP : (o + 1) * KP]
        tail = jnp.where(place == BASIS - KP + 8, 1.0, image[KP - 8 :])
        tail = jnp.where(place == UNKNOWNS - KP + 8, science[o : o + 1], tail)
        image = jnp.concatenate([image[: KP - 8], tail])
        design_ref[o] = image
        image_high, image_low = split(image)
        parts_ref[:KP, o * columns : (o + 1) * columns] = image_high
        parts_ref[KP:, o * columns : (o + 1) * columns] = image_low
    parts = parts_ref[...]
    gram = lax.dot_general(parts, parts, (((1,), (1,)), ((), ())), preferred_element_type=F32)
    half = gram[:KP] + gram[KP:]
    system = half[:, :KP] + half[:, KP:]
    down, across = iota((KP, KP), 0), iota((KP, KP), 1)
    diagonal = (down == across) & (down < UNKNOWNS)
    trace = jnp.sum(jnp.where(diagonal, system, 0.0))
    system = system + jnp.where(diagonal, RIDGE * trace / UNKNOWNS, 0.0)
    groups = [system[g : g + 8] for g in range(0, KP, 8)]
    line = iota((8, KP), 0)
    spread = spread_columns(groups, 0)
    for k in range(0, UNKNOWNS, 4):
        at, own, size = k % 8, k // 8, len(spread)
        ahead = spread_columns(groups, k + 4)
        block = [[c[own][at + i : at + i + 1] for c in spread] for i in range(size)]
        groups = eliminate(groups, block, spread, own, at, line)
        spread = [eliminate(c, block, spread, own, at, line) for c in ahead]
    system = jnp.concatenate(groups)
    fitted = jnp.where(down[:, :1] < UNKNOWNS, system[:, UNKNOWNS : UNKNOWNS + 1], 0.0)
    coefficients_ref[...] = jnp.sum(jnp.where(down == across, fitted, 0.0), axis=0, keepdims=True)[
        :, :UNKNOWNS
    ]
    for o in range(ROWS):
        model = jnp.sum(design_ref[o] * fitted, axis=0, keepdims=True)
        difference_ref[o : o + 1, :] = science[o : o + 1] - model


def call(kernel, outs, *args, **options):
    return pl.pallas_call(
        kernel,
        out_shape=[jax.ShapeDtypeStruct(shape, dtype) for shape, dtype in outs],
        name=kernel.__name__,
        compiler_params=pltpu.CompilerParams(vmem_limit_bytes=VMEM_LIMIT),
        **options,
    )(*args)


def pack(strips, strip_patch, strip_row, strip_weight, peers):
    lines, columns = strips.shape
    about = jnp.stack([x.astype(F32) for x in (strip_patch, strip_row, strip_weight)])
    return call(
        pack_kernel,
        [
            ((peers // 2, TILES, 8, LANES), BF16),
            ((1, lines), jnp.int32),
            ((LANES, lines), BF16),
            ((1, lines), F32),
        ],
        strips,
        about,
        cost_estimate=pl.CostEstimate(flops=10**9, bytes_accessed=2 * 10**6, transcendentals=0),
    )


def add_notes(payload, *parts):
    (payload,) = call(
        notes_kernel,
        [(payload.shape, BF16)],
        *parts,
        payload,
        grid=(1,),
        in_specs=[pl.BlockSpec(x.shape, lambda i: (0, 0)) for x in parts]
        + [pl.BlockSpec(memory_space=pl.ANY)],
        out_specs=[pl.BlockSpec((payload.shape[0], 1, 8, LANES), lambda i: (0, NOTES, 0, 0))],
        input_output_aliases={len(parts): 0},
    )
    return payload


def fit(odd, received, science):
    rows, columns = science.shape
    return call(
        fit_kernel,
        [((rows, columns), F32), ((1, UNKNOWNS), F32)],
        odd,
        received,
        science,
        jnp.asarray(tap_table()),
        in_specs=[pl.BlockSpec(memory_space=pltpu.SMEM)]
        + [pl.BlockSpec(memory_space=pltpu.VMEM)] * 3,
        scratch_shapes=[
            pltpu.VMEM((ROWS, KP, columns), F32),
            pltpu.VMEM((2 * KP, ROWS * columns), BF16),
        ],
    )


def body(strips, strip_patch, strip_row, strip_weight, science):
    peers = lax.axis_size("patch")
    devices = lax.axis_size("det")
    count, lines, columns = strips.shape
    up = [(i, i + 1) for i in range(devices - 1)]
    down = [(j, i) for i, j in up]
    last = strips[:, :, columns - REACH :].reshape(count * lines, REACH).T
    first = strips[:, :, :REACH].reshape(count * lines, REACH).T
    before = lax.ppermute(last, "det", up)
    after = lax.ppermute(first, "det", down)
    payload, *notes = pack(
        strips.reshape(count * lines, columns), strip_patch, strip_row, strip_weight, peers
    )
    odd = (lax.axis_index("patch") & 1).reshape(1)
    payload, odd = lax.optimization_barrier((payload, odd))
    payload = add_notes(payload, *notes, before, after)
    received = lax.all_to_all(
        payload.reshape(peers * TILES, 4, LANES), "patch", split_axis=0, concat_axis=0, tiled=True
    ).reshape(payload.shape)
    difference, coefficients = fit(odd, received, science[0])
    return (difference[None], coefficients[None])


def solution(mesh):
    placed = (P("patch", None, "det"), P("patch"), P("patch"), P("patch"), P("patch", None, "det"))
    return jax.shard_map(
        body,
        mesh=mesh,
        in_specs=placed,
        out_specs=(P("patch", None, "det"), P("patch", "det", None)),
        check_vma=False,
    )
```
